32 devices in a mesh: grp: 4 (over x, core), seq: 8 (over z, y).
Axes of the slice: x: 2, y: 2, z: 4, core: 2. Of those that a mesh axis runs over, the one named last changes fastest.
Arguments:
- tile_cls: bfloat16 [8192, 1536], P(('grp', 'seq')), may hold values from -6 to 6
- ln_gain: float32 [1536], replicated, may hold values from 0.25 to 1.75
- ln_bias: float32 [1536], replicated, may hold values from -1.5 to 1.5
- gate_weight: bfloat16 [4096, 1536], P('seq'), may hold values from -0.15625 to 0.15625
- up_weight: bfloat16 [4096, 1536], P('seq'), may hold values from -0.15625 to 0.15625
- down_weight: bfloat16 [4096, 1536], P('seq'), may hold values from -0.09375 to 0.09375
- layer_scale: float32 [1536], replicated, may hold values from 0.25 to 1.75
- final_gain: float32 [1536], replicated, may hold values from 0.25 to 1.75
- final_bias: float32 [1536], replicated, may hold values from -1.5 to 1.5
- proj_weight: bfloat16 [1536, 768], replicated, may hold values from -0.15625 to 0.15625
- proj_bias: float32 [768], replicated, may hold values from -1.5 to 1.5
- slot: int32 [8192], P(('grp', 'seq')), may hold values from 0 to 8191, as said below
- slide_lengths: int32 [4, 4], P('grp'), may hold values from 1 to 1024, 2048 in all within a row
- attn_gain: float32 [768], replicated, may hold values from 0.25 to 1.75
- attn_bias: float32 [768], replicated, may hold values from -1.5 to 1.5
- q_weight: bfloat16 [768, 768], replicated
- k_weight: bfloat16 [768, 768], replicated
- v_weight: bfloat16 [768, 768], replicated, may hold values from -0.21875 to 0.21875
- o_weight: bfloat16 [768, 768], replicated, may hold values from -0.21875 to 0.21875
Outputs:
- slide_out: bfloat16 [4, 2048, 768], P('grp', 'seq')
The draws below stay inside these ranges and needn't reach their ends.
Inputs may be any that keep to these rules, and one draw needn't show every extreme that they name: slot is a permutation of all tile positions; tile t goes to device slot[t] // 256 (grp major, then seq), row slot[t] % 256; at most 16 tiles of one device go to one device, and that count is reached. `slide_lengths`: each group's lengths add up to 2048.
All inputs are finite; a program needn't handle non-finite values.
Results may differ from the reference program's by a relative error of at most 0.014.
Values may be sent and summed in bfloat16 or wider, within the bound.
A program may use at most 128 MiB of HBM per device.

```python
import math
import jax
import jax.numpy as jnp
import numpy as np
from jax import lax

D_TILE = 1536
FF = 4096
D = 768
HEADS = 12
HEAD_DIM = 64
W_SEG = 1024
RATE = 16
SLIDES = 4
TILE_DEV = 256
TILES = 8192
SEQ_LEN = 2048
CAP = 16
N_GRP = 4


def draw_slot(key, part):
    devices = TILES // TILE_DEV
    pair_count = TILE_DEV // CAP - 1
    pieces = 1 + 2 * pair_count
    first_key, offset_key, source_key, target_key = jax.random.split(jax.random.fold_in(key, 3), 4)
    first_sizes = jax.random.randint(first_key, (pair_count,), 1, CAP)
    paired = jnp.stack([first_sizes, CAP - first_sizes], 1).reshape(-1)
    sizes = jnp.concatenate([jnp.full((1,), CAP, jnp.int32), paired.astype(jnp.int32)])
    offsets = jax.random.permutation(offset_key, devices)[:pieces].astype(jnp.int32)
    piece_of = jnp.repeat(jnp.arange(pieces, dtype=jnp.int32), sizes, total_repeat_length=TILE_DEV)
    source_perm = jax.vmap(lambda sub_key: jax.random.permutation(sub_key, TILE_DEV))(jax.random.split(source_key, devices)).astype(jnp.int32)
    target_perm = jax.vmap(lambda sub_key: jax.random.permutation(sub_key, TILE_DEV))(jax.random.split(target_key, devices)).astype(jnp.int32)
    source_ids = jnp.arange(devices, dtype=jnp.int32)[:, None]
    target_dev = (source_ids + offsets[piece_of][None, :]) % devices
    column_ids = jnp.broadcast_to(jnp.arange(TILE_DEV, dtype=jnp.int32)[None, :], (devices, TILE_DEV))
    position = target_perm[target_dev, column_ids]
    ordered = target_dev * TILE_DEV + position
    inverse = jnp.argsort(source_perm, axis=1)
    return jnp.take_along_axis(ordered, inverse, axis=1).reshape(-1).astype(jnp.int32)


def shared_base(key):
    return jax.random.normal(jax.random.fold_in(key, 7), (D, D), jnp.float32) * D ** (-0.5)


def draw_k_weight(key, part):
    return shared_base(key).astype(jnp.bfloat16)


def draw_q_weight(key, part):
    fresh = jax.random.normal(jax.random.fold_in(key, 11), (D, D), jnp.float32) * (3.0 * D ** (-0.5))
    return fresh.astype(jnp.bfloat16)


def levels(own_key, extent, cuts, least, largest):
    def one(axis_at, shards_of):
        heights = jax.random.uniform(jax.random.fold_in(jax.random.fold_in(own_key, 6), axis_at), (shards_of,), jnp.float32, least / len(cuts), largest / len(cuts))
        return jnp.repeat(jnp.exp(heights), extent[axis_at] // shards_of).reshape((-1,) + (1,) * (len(extent) - axis_at - 1))

    factor_of = one(*cuts[0])
    for cut in cuts[1:]:
        factor_of = factor_of * one(*cut)
    return factor_of


def length_profile(count, total, bound, lean):
    weights = [(1 << 20) // math.isqrt(grade ** lean) + 1 for grade in range(2, count + 1)]
    spare, holding = total - bound - (count - 1), [1] * (count - 1)
    while spare > 0:
        free = [i for i in range(count - 1) if holding[i] < bound]
        pool, remaining = sum([weights[i] for i in free]), spare
        for i in free:
            more = min(bound - holding[i], max(1, remaining * weights[i] // pool), spare)
            holding[i] = holding[i] + more
            spare = spare - more
    return np.array([bound] + holding)


def uneven_parts(stream_key, number_of, total, reach, lean):
    if number_of == 2:
        one = jax.random.randint(stream_key, (), max(1, total - reach), min(reach, total - 1) + 1)
        return jnp.stack([one, total - one])
    sizes = jnp.asarray(length_profile(number_of, total, reach, lean), jnp.int32)
    couples = (number_of - 1) // 2
    giver, sink = sizes[1:1 + 2 * couples:2], sizes[2:2 + 2 * couples:2]
    slack = jnp.minimum(giver - 1, reach - sink)
    passed = jax.random.randint(jax.random.fold_in(stream_key, 1), (couples,), 0, 1 << 20) % (slack + 1)
    sizes = sizes.at[1:1 + 2 * couples:2].set(giver - passed).at[2:2 + 2 * couples:2].set(sink + passed)
    return sizes[jax.random.permutation(jax.random.fold_in(stream_key, 2), number_of)]


def bell_draw(key, shape, spread, most, cuts=(), kind=jnp.bfloat16):
    factor_of = levels(key, shape, cuts, -0.22, 0.18) if cuts else 1.0
    drawn = jax.random.normal(key, shape, jnp.float32) * spread * factor_of
    return jnp.minimum(jnp.maximum(drawn, -most), most).astype(kind)


def setup_inputs(seed: int = 0) -> dict:
    streams_of = jax.random.split(jax.random.key(seed), 20)
    tile_cls = bell_draw(streams_of[0], (TILES, D_TILE), 1.0, 6.0, ((0, 32),))
    ln_gain = jnp.clip(1.0 + 0.15 * jax.random.normal(streams_of[1], (D_TILE,), jnp.float32), 0.25, 1.75)
    ln_bias = bell_draw(streams_of[2], (D_TILE,), 0.3, 1.5, (), jnp.float32)
    gate_weight = bell_draw(streams_of[3], (FF, D_TILE), D_TILE ** -0.5, 0.15625, ((0, 8),))
    up_weight = bell_draw(streams_of[4], (FF, D_TILE), D_TILE ** -0.5, 0.15625, ((0, 8),))
    down_weight = bell_draw(streams_of[5], (FF, D_TILE), FF ** -0.5, 0.09375, ((0, 8),))
    layer_scale = jnp.clip(1.0 + 0.15 * jax.random.normal(streams_of[6], (D_TILE,), jnp.float32), 0.25, 1.75)
    final_gain = jnp.clip(1.0 + 0.15 * jax.random.normal(streams_of[7], (D_TILE,), jnp.float32), 0.25, 1.75)
    final_bias = bell_draw(streams_of[8], (D_TILE,), 0.3, 1.5, (), jnp.float32)
    proj_weight = bell_draw(streams_of[9], (D_TILE, D), D_TILE ** -0.5, 0.15625)
    proj_bias = bell_draw(streams_of[10], (D,), 0.3, 1.5, (), jnp.float32)
    slot = draw_slot(jax.random.fold_in(streams_of[19], 71), 0)
    slide_lengths = jax.vmap(lambda own: uneven_parts(own, SLIDES, SEQ_LEN, SEQ_LEN // 2, 2))(jax.random.split(streams_of[12], N_GRP)).reshape((N_GRP, SLIDES)).astype(jnp.int32)
    attn_gain = jnp.clip(1.0 + 0.15 * jax.random.normal(streams_of[13], (D,), jnp.float32), 0.25, 1.75)
    attn_bias = bell_draw(streams_of[14], (D,), 0.3, 1.5, (), jnp.float32)
    q_weight = draw_q_weight(jax.random.fold_in(streams_of[19], 71), 0)
    k_weight = draw_k_weight(jax.random.fold_in(streams_of[19], 71), 0)
    v_weight = bell_draw(streams_of[17], (D, D), D ** -0.5, 0.21875)
    o_weight = bell_draw(streams_of[18], (D, D), D ** -0.5, 0.21875)
    return dict(tile_cls=tile_cls, ln_gain=ln_gain, ln_bias=ln_bias, gate_weight=gate_weight, up_weight=up_weight, down_weight=down_weight, layer_scale=layer_scale, final_gain=final_gain, final_bias=final_bias, proj_weight=proj_weight, proj_bias=proj_bias, slot=slot, slide_lengths=slide_lengths, attn_gain=attn_gain, attn_bias=attn_bias, q_weight=q_weight, k_weight=k_weight, v_weight=v_weight, o_weight=o_weight)


def layer_norm(values, gain_vec, bias_vector):
    average = lax.optimization_barrier(jnp.mean(values, -1, keepdims=True))
    centred = values - average
    variance = lax.optimization_barrier(jnp.mean(centred * centred, -1, keepdims=True))
    return centred * lax.rsqrt(variance + 1e-06) * gain_vec + bias_vector

def attend(queries, keys_proj, values_proj, allowed):
    scores = jnp.einsum('hqd,hkd->hqk', queries.astype(jnp.float32), keys_proj.astype(jnp.float32)) * HEAD_DIM ** (-0.5)
    row_max = lax.optimization_barrier(jnp.max(jnp.where(allowed, scores, -1e+30), -1, keepdims=True))
    weights = jnp.where(allowed, jnp.exp(scores - row_max), 0.0)
    denom_sum = lax.optimization_barrier(jnp.sum(weights, -1))
    rounded = lax.optimization_barrier(weights.astype(jnp.bfloat16)).astype(jnp.float32)
    mixed = jnp.einsum('hqk,hkd->hqd', rounded, values_proj.astype(jnp.float32)) / denom_sum[..., None]
    return (mixed, row_max[..., 0] + jnp.log(denom_sum))

def pick_dilated(array, picked):
    grid = array.reshape(picked, RATE, HEADS, HEAD_DIM)[:, :HEADS]
    return jnp.transpose(jnp.diagonal(grid, axis1=1, axis2=2), (0, 2, 1))

def combine(local_out, local_lse, far_out, far_lse, length):
    picked = length // RATE
    chosen = jnp.tile(jnp.arange(RATE)[:, None] == jnp.arange(HEADS)[None, :], (picked, 1))
    distant_output_total = jnp.broadcast_to(jnp.transpose(far_out, (1, 0, 2))[:, None], (picked, RATE, HEADS, HEAD_DIM)).reshape(length, HEADS, HEAD_DIM)
    distant_logsumexp_total = jnp.broadcast_to(jnp.transpose(far_lse)[:, None], (picked, RATE, HEADS)).reshape(length, HEADS)
    peak = jnp.where(chosen, jnp.maximum(local_lse, distant_logsumexp_total), local_lse)
    local_share = jnp.exp(local_lse - peak)
    far_share = jnp.where(chosen, jnp.exp(distant_logsumexp_total - peak), 0.0)
    mixed = (local_share[..., None] * local_out + far_share[..., None] * distant_output_total) / (local_share + far_share)[..., None]
    return mixed.reshape(length, HEADS * HEAD_DIM)

def slide_layer(embed, lengths, attn_gain, attn_bias, q_weight, k_weight, v_weight, o_weight):
    length = embed.shape[0]
    slide_ends = jnp.cumsum(lengths)
    slide_of = lax.optimization_barrier(jnp.sum((jnp.arange(length)[:, None] >= slide_ends[None, :]).astype(jnp.int32), 1))
    residual = embed.astype(jnp.float32)
    normed_seq = layer_norm(residual, attn_gain, attn_bias).astype(jnp.bfloat16)
    queries = jnp.dot(normed_seq, q_weight, preferred_element_type=jnp.float32).astype(jnp.bfloat16)
    keys_proj = jnp.dot(normed_seq, k_weight, preferred_element_type=jnp.float32).astype(jnp.bfloat16)
    values_proj = jnp.dot(normed_seq, v_weight, preferred_element_type=jnp.float32).astype(jnp.bfloat16)
    segments = length // W_SEG

    def by_segment(array):
        return jnp.transpose(array.reshape(segments, W_SEG, HEADS, HEAD_DIM), (0, 2, 1, 3))
    seg_slide = slide_of.reshape(segments, W_SEG)
    allowed = (seg_slide[:, :, None] == seg_slide[:, None, :])[:, None]
    local_out, local_lse = lax.map(lambda trio: attend(trio[0], trio[1], trio[2], trio[3]), (by_segment(queries), by_segment(keys_proj), by_segment(values_proj), allowed))
    local_out = jnp.transpose(local_out, (0, 2, 1, 3)).reshape(length, HEADS, HEAD_DIM)
    local_lse = jnp.transpose(local_lse, (0, 2, 1)).reshape(length, HEADS)
    picked = length // RATE
    selected_query = jnp.transpose(pick_dilated(queries, picked), (1, 0, 2))
    chosen_k = jnp.transpose(pick_dilated(keys_proj, picked), (1, 0, 2))
    chosen_v = jnp.transpose(pick_dilated(values_proj, picked), (1, 0, 2))
    chosen_slide = jnp.transpose(slide_of.reshape(picked, RATE)[:, :HEADS])
    far_allowed = chosen_slide[:, :, None] == chosen_slide[:, None, :]
    far_out, far_lse = attend(selected_query, chosen_k, chosen_v, far_allowed)
    attn = combine(local_out, local_lse, far_out, far_lse, length).astype(jnp.bfloat16)
    return (residual + jnp.dot(attn, o_weight, preferred_element_type=jnp.float32)).astype(jnp.bfloat16)

def reference(tile_cls, ln_gain, ln_bias, gate_weight, up_weight, down_weight, layer_scale, final_gain, final_bias, proj_weight, proj_bias, slot, slide_lengths, attn_gain, attn_bias, q_weight, k_weight, v_weight, o_weight):

    def tile_block(block_rows):
        residual = block_rows.astype(jnp.float32)
        normed = layer_norm(residual, ln_gain, ln_bias).astype(jnp.bfloat16)
        gate = jnp.dot(normed, gate_weight.T, preferred_element_type=jnp.float32)
        up_part = jnp.dot(normed, up_weight.T, preferred_element_type=jnp.float32)
        hidden = (jax.nn.silu(gate) * up_part).astype(jnp.bfloat16)
        mlp_out = jnp.dot(hidden, down_weight, preferred_element_type=jnp.float32)
        tile_out = residual + layer_scale * mlp_out
        final = layer_norm(tile_out, final_gain, final_bias).astype(jnp.bfloat16)
        return (jnp.dot(final, proj_weight, preferred_element_type=jnp.float32) + proj_bias).astype(jnp.bfloat16)
    embed = lax.map(tile_block, tile_cls.reshape(-1, TILE_DEV, D_TILE)).reshape(TILES, D)
    placed = jnp.zeros((TILES, D), jnp.bfloat16).at[slot].set(embed).reshape(N_GRP, SEQ_LEN, D)

    def one_group(group_pair):
        return slide_layer(group_pair[0], group_pair[1], attn_gain, attn_bias, q_weight, k_weight, v_weight, o_weight)
    return lax.map(one_group, (placed, slide_lengths))
```

```python
import functools

import jax
import jax.numpy as jnp
from jax import lax
from jax.experimental import pallas as pl
from jax.experimental.pallas import tpu as pltpu
from jax.sharding import PartitionSpec as P

HEADS = 12
HEAD_DIM = 64
W_SEG = 1024
RATE = 16


def crossed(block, offset):
    count = lax.axis_size("seq")
    return lax.ppermute(block, "seq", [(low, low ^ offset) for low in range(count)])


DEPTH = 4
PIECES = 4
QUAD = 4


def normalise(values, gain_vec, bias_vector):
    average = jnp.mean(values, -1, keepdims=True)
    centred = values - average
    variance = jnp.mean(centred * centred, -1, keepdims=True)
    return centred * lax.rsqrt(variance + 1e-06) * gain_vec + bias_vector


def ffn_kernel(
    across,
    cls_ref,
    ln_gain_ref,
    ln_bias_ref,
    gate_ref,
    up_ref,
    down_ref,
    scale_ref,
    final_gain_ref,
    final_bias_ref,
    proj_ref,
    proj_bias_ref,
    bucket_ref,
    out_ref,
    resid,
    tiles,
    weights,
    sums,
    right_out,
    left_out,
    right_in,
    left_in,
    embed,
    local_sem,
    tile_send,
    tile_recv,
    y_send,
    y_recv,
    x_send,
    x_recv,
    twin_send,
    twin_recv,
    right_send,
    right_recv,
    left_send,
    left_recv,
):
    seq = lax.axis_index("seq")
    grp = lax.axis_index("grp")
    z = seq // across
    y = seq % across
    member = grp % QUAD
    twin = grp + 1 - 2 * (grp % 2)
    beside = grp + 2 - 4 * (member // 2)
    last = DEPTH - 1
    has_right = z < last
    has_left = z > 0
    rows = resid.shape[0]
    piece = rows // PIECES
    count = gate_ref.shape[0]
    part = count // (2 * QUAD)
    own = (gate_ref, up_ref, down_ref)
    messages = 6 * (across - 1)

    def y_peer(r):
        return {"seq": z * across + (y + r) % across}

    barrier = pltpu.get_barrier_semaphore()

    @pl.when(has_right)
    def _():
        pl.semaphore_signal(barrier, inc=1, device_id={"seq": seq + across})

    @pl.when(has_left)
    def _():
        pl.semaphore_signal(barrier, inc=1, device_id={"seq": seq - across})

    for r in range(1, across):
        pl.semaphore_signal(barrier, inc=1, device_id=y_peer(r))
    pl.semaphore_signal(barrier, inc=1, device_id={"grp": twin})
    pl.semaphore_signal(barrier, inc=1, device_id={"grp": beside})

    cls_load = pltpu.make_async_copy(cls_ref, resid, local_sem.at[3])
    cls_load.start()
    loads = [
        pltpu.make_async_copy(own[i], weights.at[0, i], local_sem.at[i]) for i in range(3)
    ]
    for load in loads:
        load.start()
    pl.semaphore_wait(
        barrier,
        across + 1 + has_right.astype(jnp.int32) + has_left.astype(jnp.int32),
    )

    def unit_rows(who, h):
        return pl.ds(pl.multiple_of((2 * who + h) * part, part), part)

    for r in range(1, across):
        for i in range(3):
            for h in range(2):
                pltpu.make_async_remote_copy(
                    src_ref=own[i].at[unit_rows(member, h)],
                    dst_ref=weights.at[r, i, unit_rows(member, h)],
                    send_sem=y_send.at[r, i, h],
                    recv_sem=y_recv.at[r, i, h],
                    device_id=y_peer(r),
                ).start()

    def where_is(w):
        return 1 + w // 6, w // 2 % 3, w % 2

    def y_copy(w):
        r, i, h = where_is(w)
        unit = weights.at[r, i, unit_rows(member, h)]
        return pltpu.make_async_remote_copy(
            src_ref=unit,
            dst_ref=unit,
            send_sem=y_send.at[r, i, h],
            recv_sem=y_recv.at[r, i, h],
            device_id=y_peer(r),
        )

    def x_copy(w, who):
        r, i, h = where_is(w)
        unit = weights.at[r, i, unit_rows(who, h)]
        return pltpu.make_async_remote_copy(
            src_ref=unit,
            dst_ref=unit,
            send_sem=x_send.at[r, i, h],
            recv_sem=x_recv.at[r, i, h],
            device_id={"grp": beside},
        )

    def twin_copy(w, hop, who):
        r, i, h = where_is(w)
        unit = weights.at[r, i, unit_rows(who, h)]
        return pltpu.make_async_remote_copy(
            src_ref=unit,
            dst_ref=unit,
            send_sem=twin_send.at[r, i, h, hop],
            recv_sem=twin_recv.at[r, i, h, hop],
            device_id={"grp": twin},
        )

    over = (member + 2) % QUAD
    twin_member = member + 1 - 2 * (member % 2)
    twin_over = (twin_member + 2) % QUAD

    def rows_of(c):
        return pl.ds(pl.multiple_of(c * piece, piece), piece)

    cls_load.wait()

    def norm_piece(c, carry):
        values = resid[rows_of(c)].astype(jnp.float32)
        tiles[z, rows_of(c)] = normalise(
            values, ln_gain_ref[...], ln_bias_ref[...]
        ).astype(jnp.bfloat16)
        return carry

    lax.fori_loop(0, PIECES, norm_piece, 0)

    def tile_right(k, c):
        unit = tiles.at[k, rows_of(c)]
        return pltpu.make_async_remote_copy(
            src_ref=unit,
            dst_ref=unit,
            send_sem=tile_send.at[0, k, c],
            recv_sem=tile_recv.at[k, c],
            device_id={"seq": seq + across},
        )

    def tile_left(k, c):
        unit = tiles.at[k, rows_of(c)]
        return pltpu.make_async_remote_copy(
            src_ref=unit,
            dst_ref=unit,
            send_sem=tile_send.at[1, k, c],
            recv_sem=tile_recv.at[k, c],
            device_id={"seq": seq - across},
        )

    def tile_step(p):
        q = p - 2 + z
        k, c = last - q // PIECES, q % PIECES
        live = (q >= 0) & (q < PIECES * DEPTH)

        @pl.when(live & (k > z))
        def _():
            tile_left(k, c).wait_recv()

        @pl.when(live & (k >= z) & has_left)
        def _():
            tile_left(k, c).start()

        s = p + 1 - z
        m, d = s // PIECES, s % PIECES
        there = (s >= 0) & (s < PIECES * DEPTH)

        @pl.when(there & (m < z))
        def _():
            tile_right(m, d).wait_recv()

        @pl.when(there & (m <= z) & has_right)
        def _():
            tile_right(m, d).start()

    def early(p, carry):
        @pl.when((p >= 0) & (p < messages))
        def _():
            y_copy(p).wait_recv()
            x_copy(p, member).start()
            twin_copy(p, 0, member).start()

        @pl.when((p >= 1) & (p <= messages))
        def _():
            x_copy(p - 1, over).wait_recv()
            twin_copy(p - 1, 1, over).start()

        tile_step(p)
        return carry

    lax.fori_loop(-1, messages + 1, early, 0)

    for load in loads:
        load.wait()

    def settle(w, carry):
        twin_copy(w, 0, twin_member).wait_recv()
        twin_copy(w, 1, twin_over).wait_recv()
        return carry

    lax.fori_loop(0, messages, settle, 0)

    def sum_right(k, c):
        return pltpu.make_async_remote_copy(
            src_ref=right_out.at[k - 1, rows_of(c)],
            dst_ref=right_in.at[k - 1, rows_of(c)],
            send_sem=right_send.at[k - 1, c],
            recv_sem=right_recv.at[k - 1, c],
            device_id={"seq": seq + across},
        )

    def sum_left(k, c):
        return pltpu.make_async_remote_copy(
            src_ref=left_out.at[k, rows_of(c)],
            dst_ref=left_in.at[k, rows_of(c)],
            send_sem=left_send.at[k, c],
            recv_sem=left_recv.at[k, c],
            device_id={"seq": seq - across},
        )

    is_end = (z == 0) | (z == last)
    first = messages + 1
    code = jnp.where(
        z == 0,
        3 + 4 * 2 + 16 * 1,
        jnp.where(z == 1, 3 + 16 * 1 + 64 * 2, jnp.where(z == 2, 4 * 3 + 16 * 2 + 64 * 1, 4 + 16 * 2 + 64 * 3)),
    )
    end_cuts = [first, first, max(first, 10), max(first, 14), max(first, 14)]
    mid_cuts = [first, first, max(first, 8), max(first, 8), max(first, 13)]

    def pick(n, values):
        found = values[0]
        for i in range(1, len(values)):
            found = jnp.where(n == i, values[i], found)
        return found

    def late(p, carry):
        tile_step(p)
        return carry

    def one_tile(n, carry):
        low = jnp.where(is_end, pick(n, end_cuts[:-1]), pick(n, mid_cuts[:-1]))
        high = jnp.where(is_end, pick(n, end_cuts[1:]), pick(n, mid_cuts[1:]))
        lax.fori_loop(low, high, late, 0)
        k = code // pick(n, [1, 4, 16, 64]) % 4

        def shard(r, inner):
            tile = tiles[k]
            dims = (((1,), (1,)), ((), ()))
            gate = lax.dot_general(
                tile, weights[r, 0], dims, preferred_element_type=jnp.float32
            )
            up_part = lax.dot_general(
                tile, weights[r, 1], dims, preferred_element_type=jnp.float32
            )
            hidden = (gate / (1.0 + jnp.exp(-gate)) * up_part).astype(jnp.bfloat16)
            term = jnp.dot(hidden, weights[r, 2], preferred_element_type=jnp.float32)

            @pl.when(r == 0)
            def _():
                sums[k] = term

            @pl.when(r > 0)
            def _():
                sums[k] += term

            return inner

        lax.fori_loop(0, across, shard, 0)

        @pl.when((z == 0) & (k > 0))
        def _():
            right_out[k - 1] = sums[k].astype(jnp.bfloat16)
            for c in range(PIECES):
                sum_right(k, c).start()

        @pl.when((z == last) & (k < last))
        def _():
            left_out[k] = sums[k].astype(jnp.bfloat16)
            for c in range(PIECES):
                sum_left(k, c).start()

        return carry

    lax.fori_loop(0, DEPTH, one_tile, 0)

    def relay_right(k, c):
        sum_right(k, c).wait_recv()
        right_out[k - 1, rows_of(c)] = (
            sums[k, rows_of(c)] + right_in[k - 1, rows_of(c)].astype(jnp.float32)
        ).astype(jnp.bfloat16)
        sum_right(k, c).start()

    def relay_left(k, c):
        sum_left(k, c).wait_recv()
        left_out[k, rows_of(c)] = (
            sums[k, rows_of(c)] + left_in[k, rows_of(c)].astype(jnp.float32)
        ).astype(jnp.bfloat16)
        sum_left(k, c).start()

    def relay(u, carry):
        k, c = u // PIECES, u % PIECES
        v = u - 1

        @pl.when((z == 1) & (u < 2 * PIECES))
        def _():
            relay_right(last - k, c)

        @pl.when((z == 2) & (u < 2 * PIECES))
        def _():
            relay_left(k, c)

        @pl.when((z == 1) & (v >= 0) & (v < PIECES))
        def _():
            relay_left(0, v)

        @pl.when((z == 2) & (v >= 0) & (v < PIECES))
        def _():
            relay_right(last, v)

        return carry

    lax.fori_loop(0, 2 * PIECES, relay, 0)

    def finish(c, carry):
        @pl.when(has_left)
        def _():
            sum_right(z, c).wait_recv()
            sums[z, rows_of(c)] += right_in[z - 1, rows_of(c)].astype(jnp.float32)

        @pl.when(has_right)
        def _():
            sum_left(z, c).wait_recv()
            sums[z, rows_of(c)] += left_in[z, rows_of(c)].astype(jnp.float32)

        tile_out = resid[rows_of(c)].astype(jnp.float32) + scale_ref[...] * sums[z, rows_of(c)]
        final = normalise(tile_out, final_gain_ref[...], final_bias_ref[...]).astype(jnp.bfloat16)
        embed[rows_of(c)] = (
            jnp.dot(final, proj_ref[...], preferred_element_type=jnp.float32) + proj_bias_ref[...]
        ).astype(jnp.bfloat16)
        return carry

    lax.fori_loop(0, PIECES, finish, 0)
    places = lax.broadcasted_iota(jnp.int32, (out_ref.shape[0], rows), 0)
    sends = (places == bucket_ref[...]).astype(jnp.bfloat16)
    out_ref[...] = jnp.dot(sends, embed[...], preferred_element_type=jnp.float32).astype(
        jnp.bfloat16
    )

    def close_weights(w, carry):
        y_copy(w).wait_send()
        x_copy(w, member).wait_send()
        twin_copy(w, 0, member).wait_send()
        twin_copy(w, 1, over).wait_send()
        return carry

    lax.fori_loop(0, messages, close_weights, 0)

    def close_tiles(u, carry):
        k, c = u // PIECES, u % PIECES

        @pl.when(has_right & (k <= z))
        def _():
            tile_right(k, c).wait_send()

        @pl.when(has_left & (k >= z))
        def _():
            tile_left(k, c).wait_send()

        @pl.when(k > z)
        def _():
            sum_right(k, c).wait_send()

        @pl.when(k < z)
        def _():
            sum_left(k, c).wait_send()

        return carry

    lax.fori_loop(0, DEPTH * PIECES, close_tiles, 0)


def ffn_rows(
    tile_cls,
    ln_gain,
    ln_bias,
    gate_weight,
    up_weight,
    down_weight,
    layer_scale,
    final_gain,
    final_bias,
    proj_weight,
    proj_bias,
    bucket,
    places,
):
    across = lax.axis_size("seq") // DEPTH
    rows, width = tile_cls.shape
    count = gate_weight.shape[0]
    narrow = proj_weight.shape[1]
    messages = pltpu.VMEM((DEPTH - 1, rows, width), jnp.bfloat16)
    sem = pltpu.SemaphoreType.DMA
    flops = 6 * DEPTH * rows * across * count * width
    anywhere = pl.BlockSpec(memory_space=pl.ANY)
    inside = pl.BlockSpec(memory_space=pltpu.VMEM)
    return pl.pallas_call(
        functools.partial(ffn_kernel, across),
        out_shape=jax.ShapeDtypeStruct((places, narrow), jnp.bfloat16),
        in_specs=[anywhere, inside, inside, anywhere, anywhere, anywhere] + [inside] * 6,
        out_specs=inside,
        scratch_shapes=[
            pltpu.VMEM((rows, width), jnp.bfloat16),
            pltpu.VMEM((DEPTH, rows, width), jnp.bfloat16),
            pltpu.VMEM((across, 3, count, width), jnp.bfloat16),
            pltpu.VMEM((DEPTH, rows, width), jnp.float32),
            messages,
            messages,
            messages,
            messages,
            pltpu.VMEM((rows, narrow), jnp.bfloat16),
            sem((4,)),
            sem((2, DEPTH, PIECES)),
            sem((DEPTH, PIECES)),
            sem((across, 3, 2)),
            sem((across, 3, 2)),
            sem((across, 3, 2)),
            sem((across, 3, 2)),
            sem((across, 3, 2, 2)),
            sem((across, 3, 2, 2)),
            sem((DEPTH - 1, PIECES)),
            sem((DEPTH - 1, PIECES)),
            sem((DEPTH - 1, PIECES)),
            sem((DEPTH - 1, PIECES)),
        ],
        compiler_params=pltpu.CompilerParams(
            collective_id=0, has_side_effects=True, vmem_limit_bytes=48 << 20
        ),
        cost_estimate=pl.CostEstimate(
            flops=flops, bytes_accessed=6 * count * width, transcendentals=0
        ),
    )(
        tile_cls,
        ln_gain[None],
        ln_bias[None],
        gate_weight,
        up_weight,
        down_weight,
        layer_scale[None],
        final_gain[None],
        final_bias[None],
        proj_weight,
        proj_bias[None],
        bucket[None],
    )


def layer_norm(values, gain_vec, bias_vector):
    average = jnp.mean(values, -1, keepdims=True)
    centred = values - average
    variance = jnp.mean(centred * centred, -1, keepdims=True)
    return centred * lax.rsqrt(variance + 1e-06) * gain_vec + bias_vector


def pick_dilated(array):
    width = array.shape[1]
    grid = array.reshape(-1, RATE, width)
    own = jnp.arange(RATE)[:, None] == jnp.arange(width)[None, :] // HEAD_DIM
    return jnp.sum(jnp.where(own[None], grid, 0), 1, dtype=jnp.float32).astype(array.dtype)


def attention_kernel(
    ends_ref,
    query_pos_ref,
    key_pos_ref,
    far_pos_ref,
    query_ref,
    key_ref,
    value_ref,
    far_key_ref,
    far_value_ref,
    o_ref,
    resid_ref,
    out_ref,
    total,
):
    pair = pl.program_id(0)

    def slides(spots):
        return sum((spots >= ends_ref[j]).astype(jnp.int32) for j in range(ends_ref.shape[0]))

    @pl.when(pair == 0)
    def _():
        total[...] = resid_ref[...].astype(jnp.float32)

    query_pos = query_pos_ref[...]
    query_slide = slides(query_pos)
    near = query_slide == slides(key_pos_ref[...])
    query = query_ref[...] * HEAD_DIM ** (-0.5)
    lane = lax.broadcasted_iota(jnp.int32, query.shape, 1)
    dims = (((1,), (1,)), ((), ()))
    results = []
    for which in range(2):
        head = 2 * pair + which
        far = (query_slide == slides(far_pos_ref[...] + head)) & (query_pos % RATE == head)
        masked = jnp.where(lane // HEAD_DIM == which, query, jnp.zeros_like(query))
        scores = lax.dot_general(
            masked, key_ref[...], dims, preferred_element_type=jnp.float32
        )
        far_scores = lax.dot_general(
            masked, far_key_ref[...], dims, preferred_element_type=jnp.float32
        )
        scores = jnp.where(near, scores, -1e30)
        far_scores = jnp.where(far, far_scores, -1e30)
        peak = jnp.maximum(
            jnp.max(scores, -1, keepdims=True), jnp.max(far_scores, -1, keepdims=True)
        )
        share = jnp.exp(scores - peak)
        far_share = jnp.exp(far_scores - peak)
        weight = jnp.sum(share, -1, keepdims=True) + jnp.sum(far_share, -1, keepdims=True)
        mixed = jnp.dot(
            share.astype(jnp.bfloat16), value_ref[...], preferred_element_type=jnp.float32
        ) + jnp.dot(
            far_share.astype(jnp.bfloat16),
            far_value_ref[...],
            preferred_element_type=jnp.float32,
        )
        results.append(mixed / weight)
    attn = jnp.where(lane < HEAD_DIM, results[0], results[1]).astype(jnp.bfloat16)
    total[...] += jnp.dot(attn, o_ref[...], preferred_element_type=jnp.float32)

    @pl.when(pair == pl.num_programs(0) - 1)
    def _():
        out_ref[...] = total[...].astype(jnp.bfloat16)


def attend(ends, query_pos, key_pos, far_pos, queries, keys, values, far_rows, o_weight, placed):
    rows, width = placed.shape
    pairs = width // 128
    key_count, far_count = keys.shape[0], far_rows.shape[0]

    def whole(array):
        return pl.BlockSpec(array.shape, lambda j: (0, 0))

    def column(count, first=0):
        return pl.BlockSpec((count, 128), lambda j: (0, first + j))

    return pl.pallas_call(
        attention_kernel,
        out_shape=jax.ShapeDtypeStruct((rows, width), jnp.bfloat16),
        grid=(pairs,),
        in_specs=[
            pl.BlockSpec(memory_space=pltpu.SMEM),
            whole(query_pos),
            whole(key_pos),
            whole(far_pos),
            column(rows),
            column(key_count),
            column(key_count),
            column(far_count),
            column(far_count, pairs),
            pl.BlockSpec((128, width), lambda j: (j, 0)),
            whole(placed),
        ],
        out_specs=pl.BlockSpec((rows, width), lambda j: (0, 0)),
        scratch_shapes=[pltpu.VMEM((rows, width), jnp.float32)],
        compiler_params=pltpu.CompilerParams(
            dimension_semantics=("arbitrary",), vmem_limit_bytes=32 << 20
        ),
        cost_estimate=pl.CostEstimate(
            flops=8 * rows * (key_count + far_count) * width,
            bytes_accessed=4 * key_count * width,
            transcendentals=rows * (key_count + far_count) * HEADS,
        ),
    )(
        ends,
        query_pos,
        key_pos,
        far_pos,
        queries,
        keys,
        values,
        far_rows,
        far_rows,
        o_weight,
        placed,
    )


def local(
    tile_cls,
    ln_gain,
    ln_bias,
    gate_weight,
    up_weight,
    down_weight,
    layer_scale,
    final_gain,
    final_bias,
    proj_weight,
    proj_bias,
    slot,
    slide_lengths,
    attn_gain,
    attn_bias,
    q_weight,
    k_weight,
    v_weight,
    o_weight,
):
    tile_rows = tile_cls.shape[0]
    width = proj_weight.shape[1]
    seq_index = lax.axis_index("seq")
    devices = lax.axis_size("grp") * lax.axis_size("seq")
    capacity = 2 * tile_rows // devices
    here = lax.axis_index("grp") * lax.axis_size("seq") + seq_index
    slots = lax.all_gather(slot, ("grp", "seq"))
    target = slot // tile_rows
    order = jnp.arange(tile_rows, dtype=jnp.int32)
    same = (target[:, None] == target[None, :]) & (order[None, :] < order[:, None])
    bucket = target * capacity + jnp.sum(same.astype(jnp.int32), 1)
    outgoing = ffn_rows(
        tile_cls,
        ln_gain,
        ln_bias,
        gate_weight,
        up_weight,
        down_weight,
        layer_scale,
        final_gain,
        final_bias,
        proj_weight,
        proj_bias,
        bucket,
        devices * capacity,
    ).reshape(devices, capacity, width)
    mine = slots // tile_rows == here
    earlier = (order[:, None] < order[None, :]).astype(jnp.bfloat16)
    rank = jnp.dot(mine.astype(jnp.bfloat16), earlier, preferred_element_type=jnp.float32)
    picks = jnp.arange(capacity, dtype=jnp.float32)[None, :, None] == rank[:, None, :]
    found = jnp.where(picks & mine[:, None, :], slots[:, None, :] % tile_rows + 1, 0)
    arrived_place = (jnp.sum(found, 2) - 1).reshape(-1)
    incoming = lax.all_to_all(outgoing, ("grp", "seq"), split_axis=0, concat_axis=0, tiled=True)
    arrived = incoming.reshape(-1, width)
    lands = (order[:, None] == arrived_place[None, :]).astype(jnp.bfloat16)
    placed = jnp.dot(lands, arrived, preferred_element_type=jnp.float32).astype(jnp.bfloat16)
    ends = [slide_lengths[0, 0]]
    for j in range(1, slide_lengths.shape[1]):
        ends.append(ends[-1] + slide_lengths[0, j])
    slide_ends = jnp.stack(ends)

    seq_resid = placed.astype(jnp.float32)
    span = W_SEG // tile_rows
    normed_seq = layer_norm(seq_resid, attn_gain, attn_bias).astype(jnp.bfloat16)
    chosen = jnp.concatenate(
        [
            pick_dilated(
                jnp.dot(normed_seq, weight, preferred_element_type=jnp.float32).astype(
                    jnp.bfloat16
                )
            )
            for weight in (k_weight, v_weight)
        ],
        1,
    )
    sent = [crossed(chosen, r) for r in range(span, lax.axis_size("seq"))]
    block = jnp.concatenate(
        [normed_seq] + [crossed(normed_seq, r) for r in range(1, span)], 0
    )
    queries = jnp.dot(normed_seq, q_weight, preferred_element_type=jnp.float32).astype(
        jnp.bfloat16
    )
    keys_proj = jnp.dot(block, k_weight, preferred_element_type=jnp.float32).astype(jnp.bfloat16)
    values_proj = jnp.dot(block, v_weight, preferred_element_type=jnp.float32).astype(
        jnp.bfloat16
    )
    near_chosen = jnp.concatenate([pick_dilated(keys_proj), pick_dilated(values_proj)], 1)
    far_pieces = [near_chosen] + sent
    far_rows = jnp.concatenate(far_pieces, 0)

    def spots(peers, step):
        offsets = jnp.arange(0, tile_rows, step, dtype=jnp.int32)
        return jnp.concatenate([(seq_index ^ r) * tile_rows + offsets for r in peers])

    result = attend(
        slide_ends,
        spots([0], 1)[:, None],
        spots(range(span), 1)[None, :],
        spots(range(lax.axis_size("seq")), RATE)[None, :],
        queries,
        keys_proj,
        values_proj,
        far_rows,
        o_weight,
        placed,
    )
    return result[None]


def solution(mesh):
    return jax.shard_map(
        local,
        mesh=mesh,
        in_specs=(
            P(("grp", "seq"), None),
            P(),
            P(),
            P("seq", None),
            P("seq", None),
            P("seq", None),
            P(),
            P(),
            P(),
            P(),
            P(),
            P(("grp", "seq")),
            P("grp", None),
            P(),
            P(),
            P(),
            P(),
            P(),
            P(),
        ),
        out_specs=P("grp", "seq", None),
        check_vma=False,
    )
```

```python
import functools

import jax
import jax.numpy as jnp
from jax import lax
from jax.experimental import pallas as pl
from jax.experimental.pallas import tpu as pltpu
from jax.sharding import PartitionSpec as P

HEADS = 12
HEAD_DIM = 64
W_SEG = 1024
RATE = 16


def crossed(block, offset):
    count = lax.axis_size("seq")
    return lax.ppermute(block, "seq", [(low, low ^ offset) for low in range(count)])


DEPTH = 4
PIECES = 4
QUAD = 4


def normalise(values, gain_vec, bias_vector):
    average = jnp.mean(values, -1, keepdims=True)
    centred = values - average
    variance = jnp.mean(centred * centred, -1, keepdims=True)
    return centred * lax.rsqrt(variance + 1e-06) * gain_vec + bias_vector


def ffn_kernel(
    across,
    cls_ref,
    ln_gain_ref,
    ln_bias_ref,
    gate_ref,
    up_ref,
    down_ref,
    scale_ref,
    final_gain_ref,
    final_bias_ref,
    proj_ref,
    proj_bias_ref,
    slot_ref,
    attn_gain_ref,
    attn_bias_ref,
    placed_ref,
    normed_ref,
    resid,
    tiles,
    weights,
    sums,
    right_out,
    left_out,
    right_in,
    left_in,
    embed,
    outgoing,
    arrived,
    codes_out,
    codes_in,
    local_sem,
    tile_send,
    tile_recv,
    y_send,
    y_recv,
    x_send,
    x_recv,
    twin_send,
    twin_recv,
    right_send,
    right_recv,
    left_send,
    left_recv,
    code_send,
    code_recv,
    row_send,
    row_recv,
):
    seq = lax.axis_index("seq")
    grp = lax.axis_index("grp")
    z = seq // across
    y = seq % across
    member = grp % QUAD
    twin = grp + 1 - 2 * (grp % 2)
    beside = grp + 2 - 4 * (member // 2)
    last = DEPTH - 1
    has_right = z < last
    has_left = z > 0
    rows = resid.shape[0]
    piece = rows // PIECES
    count = gate_ref.shape[0]
    part = count // (2 * QUAD)
    own = (gate_ref, up_ref, down_ref)
    messages = 6 * (across - 1)

    def y_peer(r):
        return {"seq": z * across + (y + r) % across}

    seq_count = lax.axis_size("seq")
    devices = lax.axis_size("grp") * seq_count
    here = grp * seq_count + seq
    places = outgoing.shape[0]
    capacity = places // devices

    def peer(r):
        there = (here + r) % devices
        return there, {"grp": there // seq_count, "seq": there % seq_count}

    barrier = pltpu.get_barrier_semaphore()

    def greet(r, carry):
        pl.semaphore_signal(barrier, inc=1, device_id=peer(r)[1])
        return carry

    lax.fori_loop(1, devices, greet, 0)

    cls_load = pltpu.make_async_copy(cls_ref, resid, local_sem.at[3])
    cls_load.start()
    loads = [
        pltpu.make_async_copy(own[i], weights.at[0, i], local_sem.at[i]) for i in range(3)
    ]
    for load in loads:
        load.start()
    pl.semaphore_wait(barrier, devices - 1)

    def unit_rows(who, h):
        return pl.ds(pl.multiple_of((2 * who + h) * part, part), part)

    for r in range(1, across):
        for i in range(3):
            for h in range(2):
                pltpu.make_async_remote_copy(
                    src_ref=own[i].at[unit_rows(member, h)],
                    dst_ref=weights.at[r, i, unit_rows(member, h)],
                    send_sem=y_send.at[r, i, h],
                    recv_sem=y_recv.at[r, i, h],
                    device_id=y_peer(r),
                ).start()

    def where_is(w):
        return 1 + w // 6, w // 2 % 3, w % 2

    def y_copy(w):
        r, i, h = where_is(w)
        unit = weights.at[r, i, unit_rows(member, h)]
        return pltpu.make_async_remote_copy(
            src_ref=unit,
            dst_ref=unit,
            send_sem=y_send.at[r, i, h],
            recv_sem=y_recv.at[r, i, h],
            device_id=y_peer(r),
        )

    def x_copy(w, who):
        r, i, h = where_is(w)
        unit = weights.at[r, i, unit_rows(who, h)]
        return pltpu.make_async_remote_copy(
            src_ref=unit,
            dst_ref=unit,
            send_sem=x_send.at[r, i, h],
            recv_sem=x_recv.at[r, i, h],
            device_id={"grp": beside},
        )

    def twin_copy(w, hop, who):
        r, i, h = where_is(w)
        unit = weights.at[r, i, unit_rows(who, h)]
        return pltpu.make_async_remote_copy(
            src_ref=unit,
            dst_ref=unit,
            send_sem=twin_send.at[r, i, h, hop],
            recv_sem=twin_recv.at[r, i, h, hop],
            device_id={"grp": twin},
        )

    over = (member + 2) % QUAD
    twin_member = member + 1 - 2 * (member % 2)
    twin_over = (twin_member + 2) % QUAD

    def rows_of(c):
        return pl.ds(pl.multiple_of(c * piece, piece), piece)

    cls_load.wait()

    def tile_right(k, c):
        unit = tiles.at[k, rows_of(c)]
        return pltpu.make_async_remote_copy(
            src_ref=unit,
            dst_ref=unit,
            send_sem=tile_send.at[0, k, c],
            recv_sem=tile_recv.at[k, c],
            device_id={"seq": seq + across},
        )

    def tile_left(k, c):
        unit = tiles.at[k, rows_of(c)]
        return pltpu.make_async_remote_copy(
            src_ref=unit,
            dst_ref=unit,
            send_sem=tile_send.at[1, k, c],
            recv_sem=tile_recv.at[k, c],
            device_id={"seq": seq - across},
        )

    def norm_piece(c, carry):
        values = resid[rows_of(c)].astype(jnp.float32)
        tiles[z, rows_of(c)] = normalise(
            values, ln_gain_ref[...], ln_bias_ref[...]
        ).astype(jnp.bfloat16)

        @pl.when(z == 0)
        def _():
            tile_right(0, c).start()

        @pl.when(z == last)
        def _():
            tile_left(last, c).start()

        return carry

    lax.fori_loop(0, PIECES, norm_piece, 0)

    targets = slot_ref[...].reshape(1, rows) // rows
    spots = slot_ref[...].reshape(1, rows) % rows
    device_iota = lax.broadcasted_iota(jnp.int32, (devices, rows), 0)
    chosen = device_iota == targets
    before = (
        lax.broadcasted_iota(jnp.int32, (rows, rows), 0)
        < lax.broadcasted_iota(jnp.int32, (rows, rows), 1)
    ).astype(jnp.bfloat16)
    earlier = jnp.dot(chosen.astype(jnp.bfloat16), before, preferred_element_type=jnp.float32)
    rank = jnp.sum(jnp.where(chosen, earlier, 0.0), 0, keepdims=True).astype(jnp.int32)
    bucket = targets * capacity + rank
    ordinal = lax.broadcasted_iota(jnp.int32, (places, rows), 0)
    coded = jnp.where(chosen, spots + 1, 0).astype(jnp.bfloat16)
    codes = lax.dot_general(
        coded,
        (ordinal == here * capacity + rank).astype(jnp.bfloat16),
        (((1,), (1,)), ((), ())),
        preferred_element_type=jnp.float32,
    )
    for j in range(places // 128):
        codes_out[:, j, :] = codes[:, 128 * j : 128 * (j + 1)]
    codes_in[here] = codes_out[here]

    def code_copy(r):
        there, device_id = peer(r)
        return pltpu.make_async_remote_copy(
            src_ref=codes_out.at[there],
            dst_ref=codes_in.at[here],
            send_sem=code_send.at[there],
            recv_sem=code_recv.at[here],
            device_id=device_id,
        )

    def code_start(r, carry):
        code_copy(r).start()
        return carry

    lax.fori_loop(1, devices, code_start, 0)

    def tile_step(p):
        q = p - 2 + z
        k, c = last - q // PIECES, q % PIECES
        live = (q >= 0) & (q < PIECES * DEPTH)

        @pl.when(live & (k > z))
        def _():
            tile_left(k, c).wait_recv()

        @pl.when(live & (k >= z) & has_left & has_right)
        def _():
            tile_left(k, c).start()

        s = p + 1 - z
        m, d = s // PIECES, s % PIECES
        there = (s >= 0) & (s < PIECES * DEPTH)

        @pl.when(there & (m < z))
        def _():
            tile_right(m, d).wait_recv()

        @pl.when(there & (m <= z) & has_left & has_right)
        def _():
            tile_right(m, d).start()

    def settle(w, carry):
        twin_copy(w, 0, twin_member).wait_recv()
        twin_copy(w, 1, twin_over).wait_recv()
        return carry

    def sum_right(k, c):
        return pltpu.make_async_remote_copy(
            src_ref=right_out.at[k - 1, rows_of(c)],
            dst_ref=right_in.at[k - 1, rows_of(c)],
            send_sem=right_send.at[k - 1, c],
            recv_sem=right_recv.at[k - 1, c],
            device_id={"seq": seq + across},
        )

    def sum_left(k, c):
        return pltpu.make_async_remote_copy(
            src_ref=left_out.at[k, rows_of(c)],
            dst_ref=left_in.at[k, rows_of(c)],
            send_sem=left_send.at[k, c],
            recv_sem=left_recv.at[k, c],
            device_id={"seq": seq - across},
        )

    def relay_right(k, c):
        sum_right(k, c).wait_recv()
        right_out[k - 1, rows_of(c)] = (
            sums[k, rows_of(c)] + right_in[k - 1, rows_of(c)].astype(jnp.float32)
        ).astype(jnp.bfloat16)
        sum_right(k, c).start()

    def relay_left(k, c):
        sum_left(k, c).wait_recv()
        left_out[k, rows_of(c)] = (
            sums[k, rows_of(c)] + left_in[k, rows_of(c)].astype(jnp.float32)
        ).astype(jnp.bfloat16)
        sum_left(k, c).start()

    is_end = (z == 0) | (z == last)
    ready = max(6, messages)

    def pick(n, values):
        found = values[0]
        for i in range(1, len(values)):
            found = jnp.where(n == i, values[i], found)
        return found

    first = jnp.where(z < 2, last, 0)
    second = jnp.where(z == 0, 2, jnp.where(z == 1, 0, jnp.where(z == 2, last, 1)))
    third = jnp.where(z == 0, 1, jnp.where(z == 1, 2, jnp.where(z == 2, 1, 2)))
    end_plan = [
        (1, z, 0, 1),
        (5, first, 0, 1),
        (ready, first, 1, across),
        (ready + 3, second, 0, across),
        (ready + 7, third, 0, across),
        (ready + 8, z, 1, across),
    ]
    mid_plan = [
        (1, z, 0, 1),
        (4, first, 0, 1),
        (5, second, 0, 1),
        (ready, first, 1, across),
        (ready + 1, second, 1, across),
        (ready + 2, third, 0, across),
        (ready + 4, z, 1, across),
    ]

    def chosen_work(p):
        k, low, high = z, 0, 0
        for plan, live in ((end_plan, is_end), (mid_plan, ~is_end)):
            for at, tile, start, stop in plan:
                hit = live & (p == at)
                k = jnp.where(hit, tile, k)
                low = jnp.where(hit, start, low)
                high = jnp.where(hit, stop, high)
        return k, low, high

    def step(p, carry):
        @pl.when((p >= 0) & (p < messages))
        def _():
            y_copy(p).wait_recv()
            x_copy(p, member).start()
            twin_copy(p, 0, member).start()

        @pl.when((p >= 1) & (p <= messages))
        def _():
            x_copy(p - 1, over).wait_recv()
            twin_copy(p - 1, 1, over).start()

        tile_step(p)

        @pl.when(p == 0)
        def _():
            for load in loads:
                load.wait()

        @pl.when(p == ready)
        def _():
            lax.fori_loop(0, messages, settle, 0)

        u = p - ready - 2
        v = u - 1

        @pl.when((z == 1) & (u >= 0) & (u < 2 * PIECES))
        def _():
            relay_right(last - u // PIECES, u % PIECES)

        @pl.when((z == 2) & (u >= 0) & (u < 2 * PIECES))
        def _():
            relay_left(u // PIECES, u % PIECES)

        @pl.when((z == 1) & (v >= 0) & (v < PIECES))
        def _():
            relay_left(0, v)

        @pl.when((z == 2) & (v >= 0) & (v < PIECES))
        def _():
            relay_right(last, v)

        k, low, high = chosen_work(p)

        def shard(r, inner):
            tile = tiles[k]
            dims = (((1,), (1,)), ((), ()))
            gate = lax.dot_general(
                tile, weights[r, 0], dims, preferred_element_type=jnp.float32
            )
            up_part = lax.dot_general(
                tile, weights[r, 1], dims, preferred_element_type=jnp.float32
            )
            hidden = (gate / (1.0 + jnp.exp(-gate)) * up_part).astype(jnp.bfloat16)
            term = jnp.dot(hidden, weights[r, 2], preferred_element_type=jnp.float32)

            @pl.when(r == 0)
            def _():
                sums[k] = term

            @pl.when(r > 0)
            def _():
                sums[k] += term

            return inner

        lax.fori_loop(low, high, shard, 0)
        done = (low < high) & (high == across) & (k != z)

        @pl.when((z == 0) & done)
        def _():
            right_out[k - 1] = sums[k].astype(jnp.bfloat16)
            for c in range(PIECES):
                sum_right(k, c).start()

        @pl.when((z == last) & done)
        def _():
            left_out[k] = sums[k].astype(jnp.bfloat16)
            for c in range(PIECES):
                sum_left(k, c).start()

        return carry

    lax.fori_loop(-1, ready + 10, step, 0)

    def finish(c, carry):
        @pl.when(has_left)
        def _():
            sum_right(z, c).wait_recv()
            sums[z, rows_of(c)] += right_in[z - 1, rows_of(c)].astype(jnp.float32)

        @pl.when(has_right)
        def _():
            sum_left(z, c).wait_recv()
            sums[z, rows_of(c)] += left_in[z, rows_of(c)].astype(jnp.float32)

        tile_out = resid[rows_of(c)].astype(jnp.float32) + scale_ref[...] * sums[z, rows_of(c)]
        final = normalise(tile_out, final_gain_ref[...], final_bias_ref[...]).astype(jnp.bfloat16)
        embed[rows_of(c)] = (
            jnp.dot(final, proj_ref[...], preferred_element_type=jnp.float32) + proj_bias_ref[...]
        ).astype(jnp.bfloat16)
        return carry

    lax.fori_loop(0, PIECES, finish, 0)

    sends = (ordinal == bucket).astype(jnp.bfloat16)
    outgoing[...] = jnp.dot(sends, embed[...], preferred_element_type=jnp.float32).astype(
        jnp.bfloat16
    )

    def slab(device):
        return pl.ds(pl.multiple_of(device * capacity, capacity), capacity)

    def row_copy(r):
        there, device_id = peer(r)
        return pltpu.make_async_remote_copy(
            src_ref=outgoing.at[slab(there)],
            dst_ref=arrived.at[slab(here)],
            send_sem=row_send.at[there],
            recv_sem=row_recv.at[here],
            device_id=device_id,
        )

    def row_start(r, carry):
        row_copy(r).start()
        return carry

    lax.fori_loop(1, devices, row_start, 0)
    arrived[slab(here)] = outgoing[slab(here)]

    def collect(r, carry):
        there, device_id = peer(r)
        pltpu.make_async_remote_copy(
            src_ref=codes_out.at[there],
            dst_ref=codes_in.at[there],
            send_sem=code_send.at[there],
            recv_sem=code_recv.at[there],
            device_id=device_id,
        ).wait_recv()
        pltpu.make_async_remote_copy(
            src_ref=outgoing.at[slab(there)],
            dst_ref=arrived.at[slab(there)],
            send_sem=row_send.at[there],
            recv_sem=row_recv.at[there],
            device_id=device_id,
        ).wait_recv()
        return carry

    lax.fori_loop(1, devices, collect, 0)
    landing = jnp.sum(codes_in[...], 0).astype(jnp.int32) - 1
    targets_iota = lax.broadcasted_iota(jnp.int32, (rows, 128), 0)
    placed = jnp.zeros(placed_ref.shape, jnp.float32)
    for j in range(places // 128):
        lands = (targets_iota == landing[j : j + 1]).astype(jnp.bfloat16)
        placed += jnp.dot(
            lands, arrived[128 * j : 128 * (j + 1)], preferred_element_type=jnp.float32
        )
    placed_ref[...] = placed.astype(jnp.bfloat16)
    normed_ref[...] = normalise(placed, attn_gain_ref[...], attn_bias_ref[...]).astype(
        jnp.bfloat16
    )

    def close_rows(r, carry):
        code_copy(r).wait_send()
        row_copy(r).wait_send()
        return carry

    lax.fori_loop(1, devices, close_rows, 0)

    def close_weights(w, carry):
        y_copy(w).wait_send()
        x_copy(w, member).wait_send()
        twin_copy(w, 0, member).wait_send()
        twin_copy(w, 1, over).wait_send()
        return carry

    lax.fori_loop(0, messages, close_weights, 0)

    def close_tiles(u, carry):
        k, c = u // PIECES, u % PIECES

        @pl.when(has_right & (k <= z))
        def _():
            tile_right(k, c).wait_send()

        @pl.when(has_left & (k >= z))
        def _():
            tile_left(k, c).wait_send()

        @pl.when(k > z)
        def _():
            sum_right(k, c).wait_send()

        @pl.when(k < z)
        def _():
            sum_left(k, c).wait_send()

        return carry

    lax.fori_loop(0, DEPTH * PIECES, close_tiles, 0)


def placed_rows(
    tile_cls,
    ln_gain,
    ln_bias,
    gate_weight,
    up_weight,
    down_weight,
    layer_scale,
    final_gain,
    final_bias,
    proj_weight,
    proj_bias,
    slot,
    attn_gain,
    attn_bias,
):
    across = lax.axis_size("seq") // DEPTH
    devices = lax.axis_size("grp") * lax.axis_size("seq")
    rows, width = tile_cls.shape
    count = gate_weight.shape[0]
    narrow = proj_weight.shape[1]
    places = devices * max(16, 2 * rows // devices)
    messages = pltpu.VMEM((DEPTH - 1, rows, width), jnp.bfloat16)
    exchange = pltpu.VMEM((places, narrow), jnp.bfloat16)
    codes = pltpu.VMEM((devices, places // 128, 128), jnp.float32)
    sem = pltpu.SemaphoreType.DMA
    flops = 6 * DEPTH * rows * across * count * width
    anywhere = pl.BlockSpec(memory_space=pl.ANY)
    inside = pl.BlockSpec(memory_space=pltpu.VMEM)
    return pl.pallas_call(
        functools.partial(ffn_kernel, across),
        out_shape=[jax.ShapeDtypeStruct((rows, narrow), jnp.bfloat16)] * 2,
        in_specs=[anywhere, inside, inside, anywhere, anywhere, anywhere] + [inside] * 8,
        out_specs=[inside, inside],
        scratch_shapes=[
            pltpu.VMEM((rows, width), jnp.bfloat16),
            pltpu.VMEM((DEPTH, rows, width), jnp.bfloat16),
            pltpu.VMEM((across, 3, count, width), jnp.bfloat16),
            pltpu.VMEM((DEPTH, rows, width), jnp.float32),
            messages,
            messages,
            messages,
            messages,
            pltpu.VMEM((rows, narrow), jnp.bfloat16),
            exchange,
            exchange,
            codes,
            codes,
            sem((4,)),
            sem((2, DEPTH, PIECES)),
            sem((DEPTH, PIECES)),
            sem((across, 3, 2)),
            sem((across, 3, 2)),
            sem((across, 3, 2)),
            sem((across, 3, 2)),
            sem((across, 3, 2, 2)),
            sem((across, 3, 2, 2)),
            sem((DEPTH - 1, PIECES)),
            sem((DEPTH - 1, PIECES)),
            sem((DEPTH - 1, PIECES)),
            sem((DEPTH - 1, PIECES)),
            sem((devices,)),
            sem((devices,)),
            sem((devices,)),
            sem((devices,)),
        ],
        compiler_params=pltpu.CompilerParams(
            collective_id=0, has_side_effects=True, vmem_limit_bytes=60 << 20
        ),
        cost_estimate=pl.CostEstimate(
            flops=flops, bytes_accessed=6 * count * width, transcendentals=0
        ),
    )(
        tile_cls,
        ln_gain,
        ln_bias,
        gate_weight,
        up_weight,
        down_weight,
        layer_scale,
        final_gain,
        final_bias,
        proj_weight,
        proj_bias,
        slot,
        attn_gain,
        attn_bias,
    )


def pick_dilated(array):
    width = array.shape[1]
    grid = array.reshape(-1, RATE, width)
    own = jnp.arange(RATE)[:, None] == jnp.arange(width)[None, :] // HEAD_DIM
    return jnp.sum(jnp.where(own[None], grid, 0), 1, dtype=jnp.float32).astype(array.dtype)


def attention_kernel(
    ends_ref,
    query_pos_ref,
    key_pos_ref,
    far_pos_ref,
    query_ref,
    key_ref,
    value_ref,
    far_key_ref,
    far_value_ref,
    o_ref,
    resid_ref,
    out_ref,
    total,
):
    pair = pl.program_id(0)

    def slides(spots):
        return sum((spots >= ends_ref[j]).astype(jnp.int32) for j in range(ends_ref.shape[0]))

    @pl.when(pair == 0)
    def _():
        total[...] = resid_ref[...].astype(jnp.float32)

    query_pos = query_pos_ref[...]
    query_slide = slides(query_pos)
    near = query_slide == slides(key_pos_ref[...])
    query = query_ref[...] * HEAD_DIM ** (-0.5)
    lane = lax.broadcasted_iota(jnp.int32, query.shape, 1)
    dims = (((1,), (1,)), ((), ()))
    results = []
    for which in range(2):
        head = 2 * pair + which
        far = (query_slide == slides(far_pos_ref[...] + head)) & (query_pos % RATE == head)
        masked = jnp.where(lane // HEAD_DIM == which, query, jnp.zeros_like(query))
        scores = lax.dot_general(
            masked, key_ref[...], dims, preferred_element_type=jnp.float32
        )
        far_scores = lax.dot_general(
            masked, far_key_ref[...], dims, preferred_element_type=jnp.float32
        )
        scores = jnp.where(near, scores, -1e30)
        far_scores = jnp.where(far, far_scores, -1e30)
        peak = jnp.maximum(
            jnp.max(scores, -1, keepdims=True), jnp.max(far_scores, -1, keepdims=True)
        )
        share = jnp.exp(scores - peak)
        far_share = jnp.exp(far_scores - peak)
        weight = jnp.sum(share, -1, keepdims=True) + jnp.sum(far_share, -1, keepdims=True)
        mixed = jnp.dot(
            share.astype(jnp.bfloat16), value_ref[...], preferred_element_type=jnp.float32
        ) + jnp.dot(
            far_share.astype(jnp.bfloat16),
            far_value_ref[...],
            preferred_element_type=jnp.float32,
        )
        results.append(mixed / weight)
    attn = jnp.where(lane < HEAD_DIM, results[0], results[1]).astype(jnp.bfloat16)
    total[...] += jnp.dot(attn, o_ref[...], preferred_element_type=jnp.float32)

    @pl.when(pair == pl.num_programs(0) - 1)
    def _():
        out_ref[...] = total[...].astype(jnp.bfloat16)


def attend(ends, query_pos, key_pos, far_pos, queries, keys, values, far_rows, o_weight, placed):
    rows, width = placed.shape
    pairs = width // 128
    key_count, far_count = keys.shape[0], far_rows.shape[0]

    def whole(array):
        return pl.BlockSpec(array.shape, lambda j: (0, 0))

    def column(count, first=0):
        return pl.BlockSpec((count, 128), lambda j: (0, first + j))

    return pl.pallas_call(
        attention_kernel,
        out_shape=jax.ShapeDtypeStruct((rows, width), jnp.bfloat16),
        grid=(pairs,),
        in_specs=[
            pl.BlockSpec(memory_space=pltpu.SMEM),
            whole(query_pos),
            whole(key_pos),
            whole(far_pos),
            column(rows),
            column(key_count),
            column(key_count),
            column(far_count),
            column(far_count, pairs),
            pl.BlockSpec((128, width), lambda j: (j, 0)),
            whole(placed),
        ],
        out_specs=pl.BlockSpec((rows, width), lambda j: (0, 0)),
        scratch_shapes=[pltpu.VMEM((rows, width), jnp.float32)],
        compiler_params=pltpu.CompilerParams(
            dimension_semantics=("arbitrary",), vmem_limit_bytes=32 << 20
        ),
        cost_estimate=pl.CostEstimate(
            flops=8 * rows * (key_count + far_count) * width,
            bytes_accessed=4 * key_count * width,
            transcendentals=rows * (key_count + far_count) * HEADS,
        ),
    )(
        ends,
        query_pos,
        key_pos,
        far_pos,
        queries,
        keys,
        values,
        far_rows,
        far_rows,
        o_weight,
        placed,
    )


def local(
    tile_cls,
    ln_gain,
    ln_bias,
    gate_weight,
    up_weight,
    down_weight,
    layer_scale,
    final_gain,
    final_bias,
    proj_weight,
    proj_bias,
    slot,
    slide_lengths,
    attn_gain,
    attn_bias,
    q_weight,
    k_weight,
    v_weight,
    o_weight,
):
    tile_rows = tile_cls.shape[0]
    seq_index = lax.axis_index("seq")
    placed, normed_seq = placed_rows(
        tile_cls,
        ln_gain,
        ln_bias,
        gate_weight,
        up_weight,
        down_weight,
        layer_scale,
        final_gain,
        final_bias,
        proj_weight,
        proj_bias,
        slot,
        attn_gain,
        attn_bias,
    )
    ends = [slide_lengths[0, 0]]
    for j in range(1, slide_lengths.shape[1]):
        ends.append(ends[-1] + slide_lengths[0, j])
    slide_ends = jnp.stack(ends)
    span = W_SEG // tile_rows
    chosen = jnp.concatenate(
        [
            pick_dilated(
                jnp.dot(normed_seq, weight, preferred_element_type=jnp.float32).astype(
                    jnp.bfloat16
                )
            )
            for weight in (k_weight, v_weight)
        ],
        1,
    )
    sent = [crossed(chosen, r) for r in range(span, lax.axis_size("seq"))]
    block = jnp.concatenate(
        [normed_seq] + [crossed(normed_seq, r) for r in range(1, span)], 0
    )
    queries = jnp.dot(normed_seq, q_weight, preferred_element_type=jnp.float32).astype(
        jnp.bfloat16
    )
    keys_proj = jnp.dot(block, k_weight, preferred_element_type=jnp.float32).astype(jnp.bfloat16)
    values_proj = jnp.dot(block, v_weight, preferred_element_type=jnp.float32).astype(
        jnp.bfloat16
    )
    near_chosen = jnp.concatenate([pick_dilated(keys_proj), pick_dilated(values_proj)], 1)
    far_pieces = [near_chosen] + sent
    far_rows = jnp.concatenate(far_pieces, 0)

    def spots(peers, step):
        offsets = jnp.arange(0, tile_rows, step, dtype=jnp.int32)
        return jnp.concatenate([(seq_index ^ r) * tile_rows + offsets for r in peers])

    result = attend(
        slide_ends,
        spots([0], 1)[:, None],
        spots(range(span), 1)[None, :],
        spots(range(lax.axis_size("seq")), RATE)[None, :],
        queries,
        keys_proj,
        values_proj,
        far_rows,
        o_weight,
        placed,
    )
    return result[None]


def solution(mesh):
    return jax.shard_map(
        local,
        mesh=mesh,
        in_specs=(
            P(("grp", "seq"), None),
            P(),
            P(),
            P("seq", None),
            P("seq", None),
            P("seq", None),
            P(),
            P(),
            P(),
            P(),
            P(),
            P(("grp", "seq")),
            P("grp", None),
            P(),
            P(),
            P(),
            P(),
            P(),
            P(),
        ),
        out_specs=P("grp", "seq", None),
        check_vma=False,
    )
```

```python
import functools

import jax
import jax.numpy as jnp
from jax import lax
from jax.experimental import pallas as pl
from jax.experimental.pallas import tpu as pltpu
from jax.sharding import PartitionSpec as P

HEADS = 12
HEAD_DIM = 64
W_SEG = 1024
RATE = 16
DEPTH = 4
PIECES = 4
QUAD = 4


def normalise(values, gain_vec, bias_vector):
    average = jnp.mean(values, -1, keepdims=True)
    centred = values - average
    variance = jnp.mean(centred * centred, -1, keepdims=True)
    return centred * lax.rsqrt(variance + 1e-06) * gain_vec + bias_vector


def ffn_kernel(
    across,
    cls_ref,
    ln_gain_ref,
    ln_bias_ref,
    gate_ref,
    up_ref,
    down_ref,
    scale_ref,
    final_gain_ref,
    final_bias_ref,
    proj_ref,
    proj_bias_ref,
    slot_ref,
    attn_gain_ref,
    attn_bias_ref,
    lengths_ref,
    q_ref,
    k_ref,
    v_ref,
    o_ref,
    out_ref,
    resid,
    tiles,
    weights,
    sums,
    right_out,
    left_out,
    right_in,
    left_in,
    embed,
    outgoing,
    arrived,
    codes_out,
    codes_in,
    proj,
    square,
    normed,
    placed,
    queries,
    keys,
    values,
    bias,
    total,
    peak,
    weight,
    far_out,
    far_in,
    local_sem,
    tile_send,
    tile_recv,
    y_send,
    y_recv,
    x_send,
    x_recv,
    twin_send,
    twin_recv,
    right_send,
    right_recv,
    left_send,
    left_recv,
    code_send,
    code_recv,
    row_send,
    row_recv,
    near_send,
    near_recv,
    far_send,
    far_recv,
):
    seq = lax.axis_index("seq")
    grp = lax.axis_index("grp")
    z = seq // across
    y = seq % across
    member = grp % QUAD
    twin = grp + 1 - 2 * (grp % 2)
    beside = grp + 2 - 4 * (member // 2)
    last = DEPTH - 1
    has_right = z < last
    has_left = z > 0
    rows = resid.shape[0]
    piece = rows // PIECES
    count = gate_ref.shape[0]
    part = count // (2 * QUAD)
    own = (gate_ref, up_ref, down_ref)
    messages = 6 * (across - 1)

    def y_peer(r):
        return {"seq": z * across + (y + r) % across}

    seq_count = lax.axis_size("seq")
    devices = lax.axis_size("grp") * seq_count
    here = grp * seq_count + seq
    places = outgoing.shape[0]
    capacity = places // devices

    def peer(r):
        there = (here + r) % devices
        return there, {"grp": there // seq_count, "seq": there % seq_count}

    barrier = pltpu.get_barrier_semaphore()

    def greet(r, carry):
        pl.semaphore_signal(barrier, inc=1, device_id=peer(r)[1])
        return carry

    lax.fori_loop(1, devices, greet, 0)

    cls_load = pltpu.make_async_copy(cls_ref, resid, local_sem.at[3])
    cls_load.start()
    loads = [
        pltpu.make_async_copy(own[i], weights.at[0, i], local_sem.at[i]) for i in range(3)
    ]
    loads.append(pltpu.make_async_copy(proj_ref, proj, local_sem.at[4]))
    squares = (q_ref, k_ref, v_ref, o_ref)
    loads += [
        pltpu.make_async_copy(squares[i], square.at[i], local_sem.at[5 + i]) for i in range(4)
    ]
    for load in loads:
        load.start()
    pl.semaphore_wait(barrier, devices - 1)

    def unit_rows(who, h):
        return pl.ds(pl.multiple_of((2 * who + h) * part, part), part)

    for r in range(1, across):
        for i in range(3):
            for h in range(2):
                pltpu.make_async_remote_copy(
                    src_ref=own[i].at[unit_rows(member, h)],
                    dst_ref=weights.at[r, i, unit_rows(member, h)],
                    send_sem=y_send.at[r, i, h],
                    recv_sem=y_recv.at[r, i, h],
                    device_id=y_peer(r),
                ).start()

    def where_is(w):
        return 1 + w // 6, w // 2 % 3, w % 2

    def y_copy(w):
        r, i, h = where_is(w)
        unit = weights.at[r, i, unit_rows(member, h)]
        return pltpu.make_async_remote_copy(
            src_ref=unit,
            dst_ref=unit,
            send_sem=y_send.at[r, i, h],
            recv_sem=y_recv.at[r, i, h],
            device_id=y_peer(r),
        )

    def x_copy(w, who):
        r, i, h = where_is(w)
        unit = weights.at[r, i, unit_rows(who, h)]
        return pltpu.make_async_remote_copy(
            src_ref=unit,
            dst_ref=unit,
            send_sem=x_send.at[r, i, h],
            recv_sem=x_recv.at[r, i, h],
            device_id={"grp": beside},
        )

    def twin_copy(w, hop, who):
        r, i, h = where_is(w)
        unit = weights.at[r, i, unit_rows(who, h)]
        return pltpu.make_async_remote_copy(
            src_ref=unit,
            dst_ref=unit,
            send_sem=twin_send.at[r, i, h, hop],
            recv_sem=twin_recv.at[r, i, h, hop],
            device_id={"grp": twin},
        )

    over = (member + 2) % QUAD
    twin_member = member + 1 - 2 * (member % 2)
    twin_over = (twin_member + 2) % QUAD

    def rows_of(c):
        return pl.ds(pl.multiple_of(c * piece, piece), piece)

    cls_load.wait()

    def tile_right(k, c):
        unit = tiles.at[k, rows_of(c)]
        return pltpu.make_async_remote_copy(
            src_ref=unit,
            dst_ref=unit,
            send_sem=tile_send.at[0, k, c],
            recv_sem=tile_recv.at[k, c],
            device_id={"seq": seq + across},
        )

    def tile_left(k, c):
        unit = tiles.at[k, rows_of(c)]
        return pltpu.make_async_remote_copy(
            src_ref=unit,
            dst_ref=unit,
            send_sem=tile_send.at[1, k, c],
            recv_sem=tile_recv.at[k, c],
            device_id={"seq": seq - across},
        )

    def norm_piece(c, carry):
        values = resid[rows_of(c)].astype(jnp.float32)
        tiles[z, rows_of(c)] = normalise(
            values, ln_gain_ref[...], ln_bias_ref[...]
        ).astype(jnp.bfloat16)

        @pl.when(z == 0)
        def _():
            tile_right(0, c).start()

        @pl.when(z == last)
        def _():
            tile_left(last, c).start()

        return carry

    lax.fori_loop(0, PIECES, norm_piece, 0)

    targets = slot_ref[...].reshape(1, rows) // rows
    spots = slot_ref[...].reshape(1, rows) % rows
    device_iota = lax.broadcasted_iota(jnp.int32, (devices, rows), 0)
    chosen = device_iota == targets
    before = (
        lax.broadcasted_iota(jnp.int32, (rows, rows), 0)
        < lax.broadcasted_iota(jnp.int32, (rows, rows), 1)
    ).astype(jnp.bfloat16)
    earlier = jnp.dot(chosen.astype(jnp.bfloat16), before, preferred_element_type=jnp.float32)
    rank = jnp.sum(jnp.where(chosen, earlier, 0.0), 0, keepdims=True).astype(jnp.int32)
    bucket = targets * capacity + rank
    ordinal = lax.broadcasted_iota(jnp.int32, (places, rows), 0)
    coded = jnp.where(chosen, spots + 1, 0).astype(jnp.bfloat16)
    codes = lax.dot_general(
        coded,
        (ordinal == here * capacity + rank).astype(jnp.bfloat16),
        (((1,), (1,)), ((), ())),
        preferred_element_type=jnp.float32,
    )
    for j in range(places // 128):
        codes_out[:, j, :] = codes[:, 128 * j : 128 * (j + 1)]
    codes_in[here] = codes_out[here]

    def code_copy(r):
        there, device_id = peer(r)
        return pltpu.make_async_remote_copy(
            src_ref=codes_out.at[there],
            dst_ref=codes_in.at[here],
            send_sem=code_send.at[there],
            recv_sem=code_recv.at[here],
            device_id=device_id,
        )

    def code_start(r, carry):
        code_copy(r).start()
        return carry

    lax.fori_loop(1, devices, code_start, 0)

    def tile_step(p):
        q = p - 2 + z
        k, c = last - q // PIECES, q % PIECES
        live = (q >= 0) & (q < PIECES * DEPTH)

        @pl.when(live & (k > z))
        def _():
            tile_left(k, c).wait_recv()

        @pl.when(live & (k >= z) & has_left & has_right)
        def _():
            tile_left(k, c).start()

        s = p + 1 - z
        m, d = s // PIECES, s % PIECES
        there = (s >= 0) & (s < PIECES * DEPTH)

        @pl.when(there & (m < z))
        def _():
            tile_right(m, d).wait_recv()

        @pl.when(there & (m <= z) & has_left & has_right)
        def _():
            tile_right(m, d).start()

    def settle(w, carry):
        twin_copy(w, 0, twin_member).wait_recv()
        twin_copy(w, 1, twin_over).wait_recv()
        return carry

    def sum_right(k, c):
        return pltpu.make_async_remote_copy(
            src_ref=right_out.at[k - 1, rows_of(c)],
            dst_ref=right_in.at[k - 1, rows_of(c)],
            send_sem=right_send.at[k - 1, c],
            recv_sem=right_recv.at[k - 1, c],
            device_id={"seq": seq + across},
        )

    def sum_left(k, c):
        return pltpu.make_async_remote_copy(
            src_ref=left_out.at[k, rows_of(c)],
            dst_ref=left_in.at[k, rows_of(c)],
            send_sem=left_send.at[k, c],
            recv_sem=left_recv.at[k, c],
            device_id={"seq": seq - across},
        )

    def relay_right(k, c):
        sum_right(k, c).wait_recv()
        right_out[k - 1, rows_of(c)] = (
            sums[k, rows_of(c)] + right_in[k - 1, rows_of(c)].astype(jnp.float32)
        ).astype(jnp.bfloat16)
        sum_right(k, c).start()

    def relay_left(k, c):
        sum_left(k, c).wait_recv()
        left_out[k, rows_of(c)] = (
            sums[k, rows_of(c)] + left_in[k, rows_of(c)].astype(jnp.float32)
        ).astype(jnp.bfloat16)
        sum_left(k, c).start()

    is_end = (z == 0) | (z == last)
    ready = max(6, messages)

    def pick(n, values):
        found = values[0]
        for i in range(1, len(values)):
            found = jnp.where(n == i, values[i], found)
        return found

    first = jnp.where(z < 2, last, 0)
    second = jnp.where(z == 0, 2, jnp.where(z == 1, 0, jnp.where(z == 2, last, 1)))
    third = jnp.where(z == 0, 1, jnp.where(z == 1, 2, jnp.where(z == 2, 1, 2)))
    end_plan = [
        (1, z, 0, 1),
        (5, first, 0, 1),
        (ready, first, 1, across),
        (ready + 3, second, 0, across),
        (ready + 7, third, 0, across),
        (ready + 8, z, 1, across),
    ]
    mid_plan = [
        (1, z, 0, 1),
        (4, first, 0, 1),
        (5, second, 0, 1),
        (ready, first, 1, across),
        (ready + 1, second, 1, across),
        (ready + 2, third, 0, across),
        (ready + 4, z, 1, across),
    ]

    def chosen_work(p):
        k, low, high = z, 0, 0
        for plan, live in ((end_plan, is_end), (mid_plan, ~is_end)):
            for at, tile, start, stop in plan:
                hit = live & (p == at)
                k = jnp.where(hit, tile, k)
                low = jnp.where(hit, start, low)
                high = jnp.where(hit, stop, high)
        return k, low, high

    def step(p, carry):
        @pl.when((p >= 0) & (p < messages))
        def _():
            y_copy(p).wait_recv()
            x_copy(p, member).start()
            twin_copy(p, 0, member).start()

        @pl.when((p >= 1) & (p <= messages))
        def _():
            x_copy(p - 1, over).wait_recv()
            twin_copy(p - 1, 1, over).start()

        tile_step(p)

        @pl.when(p == 0)
        def _():
            for load in loads:
                load.wait()

        @pl.when(p == ready)
        def _():
            lax.fori_loop(0, messages, settle, 0)

        u = p - ready - 2
        v = u - 1

        @pl.when((z == 1) & (u >= 0) & (u < 2 * PIECES))
        def _():
            relay_right(last - u // PIECES, u % PIECES)

        @pl.when((z == 2) & (u >= 0) & (u < 2 * PIECES))
        def _():
            relay_left(u // PIECES, u % PIECES)

        @pl.when((z == 1) & (v >= 0) & (v < PIECES))
        def _():
            relay_left(0, v)

        @pl.when((z == 2) & (v >= 0) & (v < PIECES))
        def _():
            relay_right(last, v)

        k, low, high = chosen_work(p)

        def shard(r, inner):
            tile = tiles[k]
            dims = (((1,), (1,)), ((), ()))
            gate = lax.dot_general(
                tile, weights[r, 0], dims, preferred_element_type=jnp.float32
            )
            up_part = lax.dot_general(
                tile, weights[r, 1], dims, preferred_element_type=jnp.float32
            )
            hidden = (gate / (1.0 + jnp.exp(-gate)) * up_part).astype(jnp.bfloat16)
            term = jnp.dot(hidden, weights[r, 2], preferred_element_type=jnp.float32)

            @pl.when(r == 0)
            def _():
                sums[k] = term

            @pl.when(r > 0)
            def _():
                sums[k] += term

            return inner

        lax.fori_loop(low, high, shard, 0)
        done = (low < high) & (high == across) & (k != z)

        @pl.when((z == 0) & done)
        def _():
            right_out[k - 1] = sums[k].astype(jnp.bfloat16)
            for c in range(PIECES):
                sum_right(k, c).start()

        @pl.when((z == last) & done)
        def _():
            left_out[k] = sums[k].astype(jnp.bfloat16)
            for c in range(PIECES):
                sum_left(k, c).start()

        return carry

    lax.fori_loop(-1, ready + 10, step, 0)

    def finish(c, carry):
        @pl.when(has_left)
        def _():
            sum_right(z, c).wait_recv()
            sums[z, rows_of(c)] += right_in[z - 1, rows_of(c)].astype(jnp.float32)

        @pl.when(has_right)
        def _():
            sum_left(z, c).wait_recv()
            sums[z, rows_of(c)] += left_in[z, rows_of(c)].astype(jnp.float32)

        tile_out = resid[rows_of(c)].astype(jnp.float32) + scale_ref[...] * sums[z, rows_of(c)]
        final = normalise(tile_out, final_gain_ref[...], final_bias_ref[...]).astype(jnp.bfloat16)
        embed[rows_of(c)] = (
            jnp.dot(final, proj[...], preferred_element_type=jnp.float32) + proj_bias_ref[...]
        ).astype(jnp.bfloat16)
        return carry

    lax.fori_loop(0, PIECES, finish, 0)

    sends = (ordinal == bucket).astype(jnp.bfloat16)
    outgoing[...] = jnp.dot(sends, embed[...], preferred_element_type=jnp.float32).astype(
        jnp.bfloat16
    )

    def slab(device):
        return pl.ds(pl.multiple_of(device * capacity, capacity), capacity)

    def row_copy(r):
        there, device_id = peer(r)
        return pltpu.make_async_remote_copy(
            src_ref=outgoing.at[slab(there)],
            dst_ref=arrived.at[slab(here)],
            send_sem=row_send.at[there],
            recv_sem=row_recv.at[here],
            device_id=device_id,
        )

    def row_start(r, carry):
        row_copy(r).start()
        return carry

    lax.fori_loop(1, devices, row_start, 0)
    arrived[slab(here)] = outgoing[slab(here)]

    def collect(r, carry):
        there, device_id = peer(r)
        pltpu.make_async_remote_copy(
            src_ref=codes_out.at[there],
            dst_ref=codes_in.at[there],
            send_sem=code_send.at[there],
            recv_sem=code_recv.at[there],
            device_id=device_id,
        ).wait_recv()
        pltpu.make_async_remote_copy(
            src_ref=outgoing.at[slab(there)],
            dst_ref=arrived.at[slab(there)],
            send_sem=row_send.at[there],
            recv_sem=row_recv.at[there],
            device_id=device_id,
        ).wait_recv()
        return carry

    lax.fori_loop(1, devices, collect, 0)
    landing = jnp.sum(codes_in[...], 0).astype(jnp.int32) - 1
    targets_iota = lax.broadcasted_iota(jnp.int32, (rows, 128), 0)
    spread = jnp.zeros(placed.shape, jnp.float32)
    for j in range(places // 128):
        lands = (targets_iota == landing[j : j + 1]).astype(jnp.bfloat16)
        spread += jnp.dot(
            lands, arrived[128 * j : 128 * (j + 1)], preferred_element_type=jnp.float32
        )
    placed[...] = spread
    normed[0] = normalise(spread, attn_gain_ref[...], attn_bias_ref[...]).astype(jnp.bfloat16)

    half = rows // 2
    span = W_SEG // rows
    width = placed.shape[1]
    near_one = seq + 1 - 2 * (seq % 2)
    near_two = seq + 2 - 4 * (seq // 2 % 2)
    near_both = near_one + 2 - 4 * (seq // 2 % 2)

    def near_copy(source, kind, h, spot, device):
        there = pl.ds(h * half, half)
        return pltpu.make_async_remote_copy(
            src_ref=normed.at[source, there],
            dst_ref=normed.at[spot, there],
            send_sem=near_send.at[kind, h],
            recv_sem=near_recv.at[spot, h],
            device_id={"seq": device},
        )

    to_one = [near_copy(0, 0, h, 1, near_one) for h in range(2)]
    to_two = [near_copy(0, 1, h, 2, near_two) for h in range(2)]
    passed = [near_copy(1, 2, 0, 3, near_two), near_copy(2, 2, 1, 3, near_one)]
    for copy in (to_one[0], to_two[1], to_one[1], to_two[0]):
        copy.start()

    chosen_rows = rows // RATE

    def far_rows(device):
        return pl.ds(pl.multiple_of(device * chosen_rows, chosen_rows), chosen_rows)

    def far_copy(r):
        there = (seq + r) % seq_count
        return pltpu.make_async_remote_copy(
            src_ref=far_out,
            dst_ref=far_in.at[far_rows(seq)],
            send_sem=far_send.at[there],
            recv_sem=far_recv.at[seq],
            device_id={"seq": there},
        )

    def slides(spots):
        end = lengths_ref[0, 0]
        found = (spots >= end).astype(jnp.int32)
        for j in range(1, lengths_ref.shape[1]):
            end += lengths_ref[0, j]
            found += (spots >= end).astype(jnp.int32)
        return found

    query_pos = seq * rows + lax.broadcasted_iota(jnp.int32, (rows, 1), 0)
    query_slide = slides(query_pos)
    queries[...] = (
        jnp.dot(normed[0], square[0], preferred_element_type=jnp.float32).astype(jnp.bfloat16)
        * HEAD_DIM ** (-0.5)
    ).astype(jnp.bfloat16)
    total[...] = jnp.zeros_like(total)
    weight[...] = jnp.zeros_like(weight)
    peak[...] = jnp.full(peak.shape, -1e30, jnp.float32)
    pair_lane = lax.broadcasted_iota(jnp.int32, (rows, 128), 1)
    over_keys = (((1,), (1,)), ((), ()))

    def absorb(keys_of, values_of, mask_of):
        def pair_step(pair, carry):
            cols = pl.ds(pl.multiple_of(pair * 128, 128), 128)
            query = queries[:, cols]
            pair_keys, pair_values = keys_of(pair), values_of(pair)
            mixed, scale = [], []
            for which in range(2):
                head = 2 * pair + which
                own_lanes = pair_lane // HEAD_DIM == which
                scores = lax.dot_general(
                    jnp.where(own_lanes, query, jnp.zeros_like(query)),
                    pair_keys,
                    over_keys,
                    preferred_element_type=jnp.float32,
                )
                scores = mask_of(head, scores)
                old = peak[head]
                new = jnp.maximum(old, jnp.max(scores, -1, keepdims=True))
                shrink = jnp.exp(old - new)
                share = jnp.exp(scores - new)
                peak[head] = new
                weight[head] = weight[head] * shrink + jnp.sum(share, -1, keepdims=True)
                mixed.append(
                    jnp.dot(
                        share.astype(jnp.bfloat16),
                        pair_values,
                        preferred_element_type=jnp.float32,
                    )
                )
                scale.append(shrink)
            low = pair_lane < HEAD_DIM
            total[:, cols] = total[:, cols] * jnp.where(low, scale[0], scale[1]) + jnp.where(
                low, mixed[0], mixed[1]
            )
            return carry

        lax.fori_loop(0, width // 128, pair_step, 0)

    def pair_cols(pair, base=0):
        return pl.ds(pl.multiple_of(base + pair * 128, 128), 128)

    def near_block(r, carry):
        @pl.when(r == 1)
        def _():
            to_one[1].wait_recv()

        @pl.when(r == 2)
        def _():
            to_two[0].wait_recv()

        @pl.when(r == 3)
        def _():
            near_copy(0, 2, 0, 3, near_two).wait_recv()
            near_copy(0, 2, 1, 3, near_one).wait_recv()

        block = normed[r]
        keys[...] = jnp.dot(block, square[1], preferred_element_type=jnp.float32).astype(
            jnp.bfloat16
        )
        values[...] = jnp.dot(block, square[2], preferred_element_type=jnp.float32).astype(
            jnp.bfloat16
        )

        @pl.when(r == 0)
        def _():
            row = lax.broadcasted_iota(jnp.int32, (rows, width), 0)
            col = lax.broadcasted_iota(jnp.int32, (rows, width), 1)
            held = row % RATE == col // HEAD_DIM
            gather = (
                lax.broadcasted_iota(jnp.int32, (chosen_rows, rows), 0)
                == lax.broadcasted_iota(jnp.int32, (chosen_rows, rows), 1) // RATE
            ).astype(jnp.bfloat16)
            for base, array in ((0, keys), (width, values)):
                far_out[:, base : base + width] = jnp.dot(
                    gather,
                    jnp.where(held, array[...], jnp.zeros(array.shape, array.dtype)),
                    preferred_element_type=jnp.float32,
                ).astype(jnp.bfloat16)

            def far_start(j, inner):
                far_copy(j).start()
                return inner

            lax.fori_loop(1, seq_count, far_start, 0)
            far_in[far_rows(seq)] = far_out[...]

        there = jnp.where(
            r == 0, seq, jnp.where(r == 1, near_one, jnp.where(r == 2, near_two, near_both))
        )
        key_pos = there * rows + lax.broadcasted_iota(jnp.int32, (1, rows), 1)
        bias[...] = jnp.where(query_slide == slides(key_pos), 0.0, -1e30)
        absorb(
            lambda pair: keys[:, pair_cols(pair)],
            lambda pair: values[:, pair_cols(pair)],
            lambda head, scores: scores + bias[...],
        )

        @pl.when(r == 0)
        def _():
            to_one[0].wait_recv()
            passed[0].start()
            to_two[1].wait_recv()
            passed[1].start()

        return carry

    lax.fori_loop(0, span - 1, near_block, 0)

    def far_collect(r, carry):
        there = (seq + r) % seq_count
        pltpu.make_async_remote_copy(
            src_ref=far_out,
            dst_ref=far_in.at[far_rows(there)],
            send_sem=far_send.at[there],
            recv_sem=far_recv.at[there],
            device_id={"seq": there},
        ).wait_recv()
        return carry

    lax.fori_loop(1, seq_count, far_collect, 0)
    far_pos = RATE * lax.broadcasted_iota(jnp.int32, (1, far_in.shape[0]), 1)

    def far_mask(head, scores):
        seen = (query_slide == slides(far_pos + head)) & (query_pos % RATE == head)
        return jnp.where(seen, scores, -1e30)

    absorb(
        lambda pair: far_in[:, pair_cols(pair)],
        lambda pair: far_in[:, pair_cols(pair, width)],
        far_mask,
    )
    lax.fori_loop(span - 1, span, near_block, 0)

    def norm_pair(pair, carry):
        low = pair_lane < HEAD_DIM
        share = jnp.where(low, weight[2 * pair], weight[2 * pair + 1])
        queries[:, pair_cols(pair)] = (total[:, pair_cols(pair)] / share).astype(jnp.bfloat16)
        return carry

    lax.fori_loop(0, width // 128, norm_pair, 0)
    out_ref[...] = (
        placed[...] + jnp.dot(queries[...], square[3], preferred_element_type=jnp.float32)
    ).astype(jnp.bfloat16)

    for copy in to_one + to_two + passed:
        copy.wait_send()

    def close_far(r, carry):
        far_copy(r).wait_send()
        return carry

    lax.fori_loop(1, seq_count, close_far, 0)

    def close_rows(r, carry):
        code_copy(r).wait_send()
        row_copy(r).wait_send()
        return carry

    lax.fori_loop(1, devices, close_rows, 0)

    def close_weights(w, carry):
        y_copy(w).wait_send()
        x_copy(w, member).wait_send()
        twin_copy(w, 0, member).wait_send()
        twin_copy(w, 1, over).wait_send()
        return carry

    lax.fori_loop(0, messages, close_weights, 0)

    def close_tiles(u, carry):
        k, c = u // PIECES, u % PIECES

        @pl.when(has_right & (k <= z))
        def _():
            tile_right(k, c).wait_send()

        @pl.when(has_left & (k >= z))
        def _():
            tile_left(k, c).wait_send()

        @pl.when(k > z)
        def _():
            sum_right(k, c).wait_send()

        @pl.when(k < z)
        def _():
            sum_left(k, c).wait_send()

        return carry

    lax.fori_loop(0, DEPTH * PIECES, close_tiles, 0)


def slide_rows(
    tile_cls,
    ln_gain,
    ln_bias,
    gate_weight,
    up_weight,
    down_weight,
    layer_scale,
    final_gain,
    final_bias,
    proj_weight,
    proj_bias,
    slot,
    slide_lengths,
    attn_gain,
    attn_bias,
    q_weight,
    k_weight,
    v_weight,
    o_weight,
):
    seq_count = lax.axis_size("seq")
    across = seq_count // DEPTH
    devices = lax.axis_size("grp") * lax.axis_size("seq")
    rows, width = tile_cls.shape
    count = gate_weight.shape[0]
    narrow = proj_weight.shape[1]
    places = devices * max(16, 2 * rows // devices)
    messages = pltpu.VMEM((DEPTH - 1, rows, width), jnp.bfloat16)
    exchange = pltpu.VMEM((places, narrow), jnp.bfloat16)
    codes = pltpu.VMEM((devices, places // 128, 128), jnp.float32)
    sem = pltpu.SemaphoreType.DMA
    flops = 6 * DEPTH * rows * across * count * width
    anywhere = pl.BlockSpec(memory_space=pl.ANY)
    inside = pl.BlockSpec(memory_space=pltpu.VMEM)
    return pl.pallas_call(
        functools.partial(ffn_kernel, across),
        out_shape=jax.ShapeDtypeStruct((rows, narrow), jnp.bfloat16),
        in_specs=[anywhere, inside, inside, anywhere, anywhere, anywhere]
        + [inside] * 3
        + [anywhere]
        + [inside] * 4
        + [pl.BlockSpec(memory_space=pltpu.SMEM)]
        + [anywhere] * 4,
        out_specs=inside,
        scratch_shapes=[
            pltpu.VMEM((rows, width), jnp.bfloat16),
            pltpu.VMEM((DEPTH, rows, width), jnp.bfloat16),
            pltpu.VMEM((across, 3, count, width), jnp.bfloat16),
            pltpu.VMEM((DEPTH, rows, width), jnp.float32),
            messages,
            messages,
            messages,
            messages,
            pltpu.VMEM((rows, narrow), jnp.bfloat16),
            exchange,
            exchange,
            codes,
            codes,
            pltpu.VMEM((width, narrow), jnp.bfloat16),
            pltpu.VMEM((4, narrow, narrow), jnp.bfloat16),
            pltpu.VMEM((W_SEG // rows, rows, narrow), jnp.bfloat16),
            pltpu.VMEM((rows, narrow), jnp.float32),
            pltpu.VMEM((rows, narrow), jnp.bfloat16),
            pltpu.VMEM((rows, narrow), jnp.bfloat16),
            pltpu.VMEM((rows, narrow), jnp.bfloat16),
            pltpu.VMEM((rows, rows), jnp.float32),
            pltpu.VMEM((rows, narrow), jnp.float32),
            pltpu.VMEM((HEADS, rows, 1), jnp.float32),
            pltpu.VMEM((HEADS, rows, 1), jnp.float32),
            pltpu.VMEM((rows // RATE, 2 * narrow), jnp.bfloat16),
            pltpu.VMEM((seq_count * rows // RATE, 2 * narrow), jnp.bfloat16),
            sem((9,)),
            sem((2, DEPTH, PIECES)),
            sem((DEPTH, PIECES)),
            sem((across, 3, 2)),
            sem((across, 3, 2)),
            sem((across, 3, 2)),
            sem((across, 3, 2)),
            sem((across, 3, 2, 2)),
            sem((across, 3, 2, 2)),
            sem((DEPTH - 1, PIECES)),
            sem((DEPTH - 1, PIECES)),
            sem((DEPTH - 1, PIECES)),
            sem((DEPTH - 1, PIECES)),
            sem((devices,)),
            sem((devices,)),
            sem((devices,)),
            sem((devices,)),
            sem((3, 2)),
            sem((W_SEG // rows, 2)),
            sem((seq_count,)),
            sem((seq_count,)),
        ],
        compiler_params=pltpu.CompilerParams(
            collective_id=0, has_side_effects=True, vmem_limit_bytes=60 << 20
        ),
        cost_estimate=pl.CostEstimate(
            flops=flops, bytes_accessed=6 * count * width, transcendentals=0
        ),
    )(
        tile_cls,
        ln_gain,
        ln_bias,
        gate_weight,
        up_weight,
        down_weight,
        layer_scale,
        final_gain,
        final_bias,
        proj_weight,
        proj_bias,
        slot,
        attn_gain,
        attn_bias,
        slide_lengths,
        q_weight,
        k_weight,
        v_weight,
        o_weight,
    )


def local(*arrays):
    return slide_rows(*arrays)[None]


def solution(mesh):
    return jax.shard_map(
        local,
        mesh=mesh,
        in_specs=(
            P(("grp", "seq"), None),
            P(),
            P(),
            P("seq", None),
            P("seq", None),
            P("seq", None),
            P(),
            P(),
            P(),
            P(),
            P(),
            P(("grp", "seq")),
            P("grp", None),
            P(),
            P(),
            P(),
            P(),
            P(),
            P(),
        ),
        out_specs=P("grp", "seq", None),
        check_vma=False,
    )
```

```python
import functools

import jax
import jax.numpy as jnp
from jax import lax
from jax.experimental import pallas as pl
from jax.experimental.pallas import tpu as pltpu
from jax.sharding import PartitionSpec as P

HEADS = 12
HEAD_DIM = 64
W_SEG = 1024
RATE = 16
DEPTH = 4
PIECES = 4
QUAD = 4


def normalise(values, gain_vec, bias_vector):
    average = jnp.mean(values, -1, keepdims=True)
    centred = values - average
    variance = jnp.mean(centred * centred, -1, keepdims=True)
    return centred * lax.rsqrt(variance + 1e-06) * gain_vec + bias_vector


def ffn_kernel(
    across,
    cls_ref,
    ln_gain_ref,
    ln_bias_ref,
    gate_ref,
    up_ref,
    down_ref,
    scale_ref,
    final_gain_ref,
    final_bias_ref,
    proj_ref,
    proj_bias_ref,
    slot_ref,
    attn_gain_ref,
    attn_bias_ref,
    lengths_ref,
    q_ref,
    k_ref,
    v_ref,
    o_ref,
    out_ref,
    resid,
    tiles,
    weights,
    sums,
    right_out,
    left_out,
    right_in,
    left_in,
    embed,
    outgoing,
    arrived,
    codes_out,
    codes_in,
    bucket,
    proj,
    square,
    normed,
    placed,
    queries,
    keys,
    values,
    bias,
    total,
    peak,
    weight,
    far_out,
    far_in,
    local_sem,
    tile_send,
    tile_recv,
    y_send,
    y_recv,
    x_send,
    x_recv,
    twin_send,
    twin_recv,
    right_send,
    right_recv,
    left_send,
    left_recv,
    code_send,
    code_recv,
    row_send,
    row_recv,
    near_send,
    near_recv,
    far_send,
    far_recv,
):
    seq = lax.axis_index("seq")
    grp = lax.axis_index("grp")
    z = seq // across
    y = seq % across
    member = grp % QUAD
    twin = grp + 1 - 2 * (grp % 2)
    beside = grp + 2 - 4 * (member // 2)
    last = DEPTH - 1
    has_right = z < last
    has_left = z > 0
    rows = resid.shape[0]
    piece = rows // PIECES
    count = gate_ref.shape[0]
    part = count // (2 * QUAD)
    own = (gate_ref, up_ref, down_ref)
    messages = 6 * (across - 1)

    def y_peer(r):
        return {"seq": z * across + (y + r) % across}

    seq_count = lax.axis_size("seq")
    devices = lax.axis_size("grp") * seq_count
    here = grp * seq_count + seq
    places = outgoing.shape[0]
    capacity = places // devices

    def peer(r):
        there = (here + r) % devices
        return there, {"grp": there // seq_count, "seq": there % seq_count}

    barrier = pltpu.get_barrier_semaphore()

    def greet(r, carry):
        pl.semaphore_signal(barrier, inc=1, device_id=peer(r)[1])
        return carry

    lax.fori_loop(1, devices, greet, 0)

    cls_load = pltpu.make_async_copy(cls_ref, resid, local_sem.at[3])
    cls_load.start()
    loads = [
        pltpu.make_async_copy(own[i], weights.at[0, i], local_sem.at[i]) for i in range(3)
    ]
    loads.append(pltpu.make_async_copy(proj_ref, proj, local_sem.at[4]))
    squares = (q_ref, k_ref, v_ref, o_ref)
    loads += [
        pltpu.make_async_copy(squares[i], square.at[i], local_sem.at[5 + i]) for i in range(4)
    ]
    for load in loads:
        load.start()

    def unit_rows(who, h):
        return pl.ds(pl.multiple_of((2 * who + h) * part, part), part)

    def where_is(w):
        return 1 + w // 6, w // 2 % 3, w % 2

    def y_copy(w):
        r, i, h = where_is(w)
        unit = weights.at[r, i, unit_rows(member, h)]
        return pltpu.make_async_remote_copy(
            src_ref=unit,
            dst_ref=unit,
            send_sem=y_send.at[r, i, h],
            recv_sem=y_recv.at[r, i, h],
            device_id=y_peer(r),
        )

    def x_copy(w, who):
        r, i, h = where_is(w)
        unit = weights.at[r, i, unit_rows(who, h)]
        return pltpu.make_async_remote_copy(
            src_ref=unit,
            dst_ref=unit,
            send_sem=x_send.at[r, i, h],
            recv_sem=x_recv.at[r, i, h],
            device_id={"grp": beside},
        )

    def twin_copy(w, hop, who):
        r, i, h = where_is(w)
        unit = weights.at[r, i, unit_rows(who, h)]
        return pltpu.make_async_remote_copy(
            src_ref=unit,
            dst_ref=unit,
            send_sem=twin_send.at[r, i, h, hop],
            recv_sem=twin_recv.at[r, i, h, hop],
            device_id={"grp": twin},
        )

    over = (member + 2) % QUAD
    twin_member = member + 1 - 2 * (member % 2)
    twin_over = (twin_member + 2) % QUAD

    def rows_of(c):
        return pl.ds(pl.multiple_of(c * piece, piece), piece)

    cls_load.wait()

    def tile_right(k, c):
        unit = tiles.at[k, rows_of(c)]
        return pltpu.make_async_remote_copy(
            src_ref=unit,
            dst_ref=unit,
            send_sem=tile_send.at[0, k, c],
            recv_sem=tile_recv.at[k, c],
            device_id={"seq": seq + across},
        )

    def tile_left(k, c):
        unit = tiles.at[k, rows_of(c)]
        return pltpu.make_async_remote_copy(
            src_ref=unit,
            dst_ref=unit,
            send_sem=tile_send.at[1, k, c],
            recv_sem=tile_recv.at[k, c],
            device_id={"seq": seq - across},
        )

    def norm_piece(c, carry):
        values = resid[rows_of(c)].astype(jnp.float32)
        tiles[z, rows_of(c)] = normalise(
            values, ln_gain_ref[...], ln_bias_ref[...]
        ).astype(jnp.bfloat16)
        return carry

    lax.fori_loop(0, PIECES, norm_piece, 0)
    pl.semaphore_wait(barrier, devices - 1)

    for r in range(1, across):
        for i in range(3):
            for h in range(2):
                pltpu.make_async_remote_copy(
                    src_ref=own[i].at[unit_rows(member, h)],
                    dst_ref=weights.at[r, i, unit_rows(member, h)],
                    send_sem=y_send.at[r, i, h],
                    recv_sem=y_recv.at[r, i, h],
                    device_id=y_peer(r),
                ).start()

    for c in range(PIECES):

        @pl.when((z == 0) | (has_right & (c < z)))
        def _():
            tile_right(z, c).start()

        @pl.when((z == last) | (has_left & (c < last - z)))
        def _():
            tile_left(z, c).start()

    targets = slot_ref[...].reshape(1, rows) // rows
    spots = slot_ref[...].reshape(1, rows) % rows
    ordinal = lax.broadcasted_iota(jnp.int32, (places, rows), 0)
    def code_copy(r):
        there, device_id = peer(r)
        return pltpu.make_async_remote_copy(
            src_ref=codes_out.at[there],
            dst_ref=codes_in.at[here],
            send_sem=code_send.at[there],
            recv_sem=code_recv.at[here],
            device_id=device_id,
        )

    def code_start(r, carry):
        code_copy(r).start()
        return carry

    def send_codes():
        device_iota = lax.broadcasted_iota(jnp.int32, (devices, rows), 0)
        chosen = device_iota == targets
        before = (
            lax.broadcasted_iota(jnp.int32, (rows, rows), 0)
            < lax.broadcasted_iota(jnp.int32, (rows, rows), 1)
        ).astype(jnp.bfloat16)
        earlier = jnp.dot(chosen.astype(jnp.bfloat16), before, preferred_element_type=jnp.float32)
        rank = jnp.sum(jnp.where(chosen, earlier, 0.0), 0, keepdims=True).astype(jnp.int32)
        bucket[...] = targets * capacity + rank
        coded = jnp.where(chosen, spots + 1, 0).astype(jnp.bfloat16)
        codes = lax.dot_general(
            coded,
            (ordinal == here * capacity + rank).astype(jnp.bfloat16),
            (((1,), (1,)), ((), ())),
            preferred_element_type=jnp.float32,
        )
        for j in range(places // 128):
            codes_out[:, j, :] = codes[:, 128 * j : 128 * (j + 1)]
        codes_in[here] = codes_out[here]
        lax.fori_loop(1, devices, code_start, 0)

    def tile_step(p):
        q = p - 2 + z
        k, c = last - q // PIECES, q % PIECES
        live = (q >= 0) & (q < PIECES * DEPTH)

        @pl.when(live & (k > z))
        def _():
            tile_left(k, c).wait_recv()

        @pl.when(live & (k > z) & has_left)
        def _():
            tile_left(k, c).start()

        @pl.when(live & (k == z) & (c == 0) & has_left & has_right)
        def _():
            for e in range(PIECES):

                @pl.when(e >= last - z)
                def _():
                    tile_left(z, e).start()

        s = p + 1 - z
        m, d = s // PIECES, s % PIECES
        there = (s >= 0) & (s < PIECES * DEPTH)

        @pl.when(there & (m < z))
        def _():
            tile_right(m, d).wait_recv()

        @pl.when(there & (m < z) & has_right)
        def _():
            tile_right(m, d).start()

        @pl.when(there & (m == z) & (d == 0) & has_left & has_right)
        def _():
            for e in range(PIECES):

                @pl.when(e >= z)
                def _():
                    tile_right(z, e).start()

    def settle(w, carry):
        twin_copy(w, 0, twin_member).wait_recv()
        twin_copy(w, 1, twin_over).wait_recv()
        return carry

    def sum_right(k, c):
        return pltpu.make_async_remote_copy(
            src_ref=right_out.at[k - 1, rows_of(c)],
            dst_ref=right_in.at[k - 1, rows_of(c)],
            send_sem=right_send.at[k - 1, c],
            recv_sem=right_recv.at[k - 1, c],
            device_id={"seq": seq + across},
        )

    def sum_left(k, c):
        return pltpu.make_async_remote_copy(
            src_ref=left_out.at[k, rows_of(c)],
            dst_ref=left_in.at[k, rows_of(c)],
            send_sem=left_send.at[k, c],
            recv_sem=left_recv.at[k, c],
            device_id={"seq": seq - across},
        )

    def relay_right(k, c):
        sum_right(k, c).wait_recv()
        right_out[k - 1, rows_of(c)] = (
            sums[k, rows_of(c)] + right_in[k - 1, rows_of(c)].astype(jnp.float32)
        ).astype(jnp.bfloat16)
        sum_right(k, c).start()

    def relay_left(k, c):
        sum_left(k, c).wait_recv()
        left_out[k, rows_of(c)] = (
            sums[k, rows_of(c)] + left_in[k, rows_of(c)].astype(jnp.float32)
        ).astype(jnp.bfloat16)
        sum_left(k, c).start()

    is_end = (z == 0) | (z == last)
    ready = max(6, messages)

    def pick(n, values):
        found = values[0]
        for i in range(1, len(values)):
            found = jnp.where(n == i, values[i], found)
        return found

    first = jnp.where(z < 2, last, 0)
    second = jnp.where(z == 0, 2, jnp.where(z == 1, 0, jnp.where(z == 2, last, 1)))
    third = jnp.where(z == 0, 1, jnp.where(z == 1, 2, jnp.where(z == 2, 1, 2)))
    end_plan = [
        (1, z, 0, 1),
        (5, first, 0, 1),
        (ready, first, 1, across),
        (ready + 3, second, 0, across),
        (ready + 7, third, 0, across),
        (ready + 8, z, 1, across),
    ]
    mid_plan = [
        (1, z, 0, 1),
        (4, first, 0, 1),
        (5, second, 0, 1),
        (ready, first, 1, across),
        (ready + 1, second, 1, across),
        (ready + 2, third, 0, across),
        (ready + 4, z, 1, across),
    ]

    def chosen_work(p):
        k, low, high = z, 0, 0
        for plan, live in ((end_plan, is_end), (mid_plan, ~is_end)):
            for at, tile, start, stop in plan:
                hit = live & (p == at)
                k = jnp.where(hit, tile, k)
                low = jnp.where(hit, start, low)
                high = jnp.where(hit, stop, high)
        return k, low, high

    def step(p, carry):
        @pl.when((p >= 0) & (p < messages))
        def _():
            y_copy(p).wait_recv()
            x_copy(p, member).start()
            twin_copy(p, 0, member).start()

        @pl.when((p >= 1) & (p <= messages))
        def _():
            x_copy(p - 1, over).wait_recv()
            twin_copy(p - 1, 1, over).start()

        tile_step(p)

        @pl.when(p == 0)
        def _():
            for load in loads:
                load.wait()

            send_codes()

        @pl.when(p == ready)
        def _():
            lax.fori_loop(0, messages, settle, 0)

        u = p - ready - 2
        v = u - 1

        @pl.when((z == 1) & (u >= 0) & (u < 2 * PIECES))
        def _():
            relay_right(last - u // PIECES, u % PIECES)

        @pl.when((z == 2) & (u >= 0) & (u < 2 * PIECES))
        def _():
            relay_left(u // PIECES, u % PIECES)

        @pl.when((z == 1) & (v >= 0) & (v < PIECES))
        def _():
            relay_left(0, v)

        @pl.when((z == 2) & (v >= 0) & (v < PIECES))
        def _():
            relay_right(last, v)

        k, low, high = chosen_work(p)

        def shard(r, inner):
            tile = tiles[k]
            dims = (((1,), (1,)), ((), ()))
            gate = lax.dot_general(
                tile, weights[r, 0], dims, preferred_element_type=jnp.float32
            )
            up_part = lax.dot_general(
                tile, weights[r, 1], dims, preferred_element_type=jnp.float32
            )
            hidden = (gate / (1.0 + jnp.exp(-gate)) * up_part).astype(jnp.bfloat16)
            term = jnp.dot(hidden, weights[r, 2], preferred_element_type=jnp.float32)

            @pl.when(r == 0)
            def _():
                sums[k] = term

            @pl.when(r > 0)
            def _():
                sums[k] += term

            return inner

        lax.fori_loop(low, high, shard, 0)
        done = (low < high) & (high == across) & (k != z)

        @pl.when((z == 0) & done)
        def _():
            right_out[k - 1] = sums[k].astype(jnp.bfloat16)
            for c in range(PIECES):
                sum_right(k, c).start()

        @pl.when((z == last) & done)
        def _():
            left_out[k] = sums[k].astype(jnp.bfloat16)
            for c in range(PIECES):
                sum_left(k, c).start()

        return carry

    lax.fori_loop(-1, ready + 10, step, 0)

    def finish(c, carry):
        @pl.when(has_left)
        def _():
            sum_right(z, c).wait_recv()
            sums[z, rows_of(c)] += right_in[z - 1, rows_of(c)].astype(jnp.float32)

        @pl.when(has_right)
        def _():
            sum_left(z, c).wait_recv()
            sums[z, rows_of(c)] += left_in[z, rows_of(c)].astype(jnp.float32)

        tile_out = resid[rows_of(c)].astype(jnp.float32) + scale_ref[...] * sums[z, rows_of(c)]
        final = normalise(tile_out, final_gain_ref[...], final_bias_ref[...]).astype(jnp.bfloat16)
        embed[rows_of(c)] = (
            jnp.dot(final, proj[...], preferred_element_type=jnp.float32) + proj_bias_ref[...]
        ).astype(jnp.bfloat16)
        return carry

    lax.fori_loop(0, PIECES, finish, 0)

    sends = (ordinal == bucket[...]).astype(jnp.bfloat16)
    outgoing[...] = jnp.dot(sends, embed[...], preferred_element_type=jnp.float32).astype(
        jnp.bfloat16
    )

    def slab(device):
        return pl.ds(pl.multiple_of(device * capacity, capacity), capacity)

    def row_copy(r):
        there, device_id = peer(r)
        return pltpu.make_async_remote_copy(
            src_ref=outgoing.at[slab(there)],
            dst_ref=arrived.at[slab(here)],
            send_sem=row_send.at[there],
            recv_sem=row_recv.at[here],
            device_id=device_id,
        )

    def row_start(r, carry):
        row_copy(r).start()
        return carry

    lax.fori_loop(1, devices, row_start, 0)
    arrived[slab(here)] = outgoing[slab(here)]

    def collect(r, carry):
        there, device_id = peer(r)
        pltpu.make_async_remote_copy(
            src_ref=codes_out.at[there],
            dst_ref=codes_in.at[there],
            send_sem=code_send.at[there],
            recv_sem=code_recv.at[there],
            device_id=device_id,
        ).wait_recv()
        pltpu.make_async_remote_copy(
            src_ref=outgoing.at[slab(there)],
            dst_ref=arrived.at[slab(there)],
            send_sem=row_send.at[there],
            recv_sem=row_recv.at[there],
            device_id=device_id,
        ).wait_recv()
        return carry

    lax.fori_loop(1, devices, collect, 0)
    landing = jnp.sum(codes_in[...], 0).astype(jnp.int32) - 1
    targets_iota = lax.broadcasted_iota(jnp.int32, (rows, 128), 0)
    spread = jnp.zeros(placed.shape, jnp.float32)
    for j in range(places // 128):
        lands = (targets_iota == landing[j : j + 1]).astype(jnp.bfloat16)
        spread += jnp.dot(
            lands, arrived[128 * j : 128 * (j + 1)], preferred_element_type=jnp.float32
        )
    placed[...] = spread
    normed[0] = normalise(spread, attn_gain_ref[...], attn_bias_ref[...]).astype(jnp.bfloat16)

    half = rows // 2
    span = W_SEG // rows
    width = placed.shape[1]
    near_one = seq + 1 - 2 * (seq % 2)
    near_two = seq + 2 - 4 * (seq // 2 % 2)
    near_both = near_one + 2 - 4 * (seq // 2 % 2)

    def near_copy(source, kind, h, spot, device):
        there = pl.ds(h * half, half)
        return pltpu.make_async_remote_copy(
            src_ref=normed.at[source, there],
            dst_ref=normed.at[spot, there],
            send_sem=near_send.at[kind, h],
            recv_sem=near_recv.at[spot, h],
            device_id={"seq": device},
        )

    to_one = [near_copy(0, 0, h, 1, near_one) for h in range(2)]
    to_two = [near_copy(0, 1, h, 2, near_two) for h in range(2)]
    passed = [near_copy(1, 2, 0, 3, near_two), near_copy(2, 2, 1, 3, near_one)]
    for copy in (to_one[0], to_two[1], to_one[1], to_two[0]):
        copy.start()

    chosen_rows = rows // RATE

    def far_rows(device):
        return pl.ds(pl.multiple_of(device * chosen_rows, chosen_rows), chosen_rows)

    blocks = seq_count // span
    strangers = seq_count - span

    def stranger(j):
        return (seq // span + 1 + j // span) % blocks * span + (seq + j) % span

    def far_copy(r):
        there = stranger(r)
        return pltpu.make_async_remote_copy(
            src_ref=far_out,
            dst_ref=far_in.at[far_rows(seq)],
            send_sem=far_send.at[there],
            recv_sem=far_recv.at[seq],
            device_id={"seq": there},
        )

    def slides(spots):
        end = lengths_ref[0, 0]
        found = (spots >= end).astype(jnp.int32)
        for j in range(1, lengths_ref.shape[1]):
            end += lengths_ref[0, j]
            found += (spots >= end).astype(jnp.int32)
        return found

    query_pos = seq * rows + lax.broadcasted_iota(jnp.int32, (1, rows), 1)
    query_slide = slides(query_pos)
    queries[...] = (
        jnp.dot(normed[0], square[0], preferred_element_type=jnp.float32).astype(jnp.bfloat16)
        * HEAD_DIM ** (-0.5)
    ).astype(jnp.bfloat16)
    total[...] = jnp.zeros_like(total)
    weight[...] = jnp.zeros_like(weight)
    peak[...] = jnp.full(peak.shape, -1e30, jnp.float32)
    pair_lane = lax.broadcasted_iota(jnp.int32, (rows, 128), 1)
    over_keys = (((1,), (1,)), ((), ()))

    def absorb(keys_of, values_of, mask_of):
        def pair_step(pair, carry):
            cols = pl.ds(pl.multiple_of(pair * 128, 128), 128)
            query = queries[:, cols]
            pair_keys = keys_of(pair)
            turned = jnp.transpose(values_of(pair))
            for which in range(2):
                head = 2 * pair + which
                own_lanes = pair_lane // HEAD_DIM == which
                scores = lax.dot_general(
                    pair_keys,
                    jnp.where(own_lanes, query, jnp.zeros_like(query)),
                    over_keys,
                    preferred_element_type=jnp.float32,
                )
                scores = mask_of(head, scores)
                old = peak[head]
                new = jnp.maximum(old, jnp.max(scores, 0, keepdims=True))
                shrink = jnp.exp(old - new)
                share = jnp.exp(scores - new)
                peak[head] = new
                weight[head] = weight[head] * shrink + jnp.sum(share, 0, keepdims=True)
                mixed = jnp.dot(
                    turned[HEAD_DIM * which : HEAD_DIM * (which + 1)],
                    share.astype(jnp.bfloat16),
                    preferred_element_type=jnp.float32,
                )
                total[head] = total[head] * shrink + mixed
            return carry

        lax.fori_loop(0, width // 128, pair_step, 0, unroll=2)

    def pair_cols(pair, base=0):
        return pl.ds(pl.multiple_of(base + pair * 128, 128), 128)

    def near_block(r, carry):
        @pl.when(r == 1)
        def _():
            to_one[1].wait_recv()

        @pl.when(r == 2)
        def _():
            to_two[0].wait_recv()

        @pl.when(r == 3)
        def _():
            near_copy(0, 2, 0, 3, near_two).wait_recv()
            near_copy(0, 2, 1, 3, near_one).wait_recv()

        block = normed[r]
        keys[...] = jnp.dot(block, square[1], preferred_element_type=jnp.float32).astype(
            jnp.bfloat16
        )
        values[...] = jnp.dot(block, square[2], preferred_element_type=jnp.float32).astype(
            jnp.bfloat16
        )

        there = jnp.where(
            r == 0, seq, jnp.where(r == 1, near_one, jnp.where(r == 2, near_two, near_both))
        )
        row = lax.broadcasted_iota(jnp.int32, (rows, width), 0)
        col = lax.broadcasted_iota(jnp.int32, (rows, width), 1)
        held = row % RATE == col // HEAD_DIM
        gather = (
            lax.broadcasted_iota(jnp.int32, (chosen_rows, rows), 0)
            == lax.broadcasted_iota(jnp.int32, (chosen_rows, rows), 1) // RATE
        ).astype(jnp.bfloat16)
        for base, array in ((0, keys), (width, values)):
            far_in[far_rows(there), base : base + width] = jnp.dot(
                gather,
                jnp.where(held, array[...], jnp.zeros(array.shape, array.dtype)),
                preferred_element_type=jnp.float32,
            ).astype(jnp.bfloat16)

        @pl.when(r == 0)
        def _():
            far_out[...] = far_in[far_rows(seq)]

            def far_start(j, inner):
                far_copy(j).start()
                return inner

            lax.fori_loop(0, strangers, far_start, 0)

        key_pos = there * rows + lax.broadcasted_iota(jnp.int32, (rows, 1), 0)
        bias[...] = jnp.where(query_slide == slides(key_pos), 0.0, -1e30)
        absorb(
            lambda pair: keys[:, pair_cols(pair)],
            lambda pair: values[:, pair_cols(pair)],
            lambda head, scores: scores + bias[...],
        )

        @pl.when(r == 0)
        def _():
            to_one[0].wait_recv()
            passed[0].start()
            to_two[1].wait_recv()
            passed[1].start()

        return carry

    lax.fori_loop(0, span, near_block, 0)

    def far_collect(r, carry):
        there = stranger(r)
        pltpu.make_async_remote_copy(
            src_ref=far_out,
            dst_ref=far_in.at[far_rows(there)],
            send_sem=far_send.at[there],
            recv_sem=far_recv.at[there],
            device_id={"seq": there},
        ).wait_recv()
        return carry

    lax.fori_loop(0, strangers, far_collect, 0)
    far_pos = RATE * lax.broadcasted_iota(jnp.int32, (far_in.shape[0], 1), 0)

    def far_mask(head, scores):
        seen = (query_slide == slides(far_pos + head)) & (query_pos % RATE == head)
        return jnp.where(seen, scores, -1e30)

    absorb(
        lambda pair: far_in[:, pair_cols(pair)],
        lambda pair: far_in[:, pair_cols(pair, width)],
        far_mask,
    )

    attn = (total[...] / weight[...]).astype(jnp.bfloat16).reshape(width, rows)
    out_ref[...] = (
        placed[...]
        + lax.dot_general(
            attn, square[3], (((0,), (0,)), ((), ())), preferred_element_type=jnp.float32
        )
    ).astype(jnp.bfloat16)

    for copy in to_one + to_two + passed:
        copy.wait_send()

    def close_far(r, carry):
        far_copy(r).wait_send()
        return carry

    lax.fori_loop(0, strangers, close_far, 0)

    def close_rows(r, carry):
        code_copy(r).wait_send()
        row_copy(r).wait_send()
        return carry

    lax.fori_loop(1, devices, close_rows, 0)

    def close_weights(w, carry):
        y_copy(w).wait_send()
        x_copy(w, member).wait_send()
        twin_copy(w, 0, member).wait_send()
        twin_copy(w, 1, over).wait_send()
        return carry

    lax.fori_loop(0, messages, close_weights, 0)

    def close_tiles(u, carry):
        k, c = u // PIECES, u % PIECES

        @pl.when(has_right & (k <= z))
        def _():
            tile_right(k, c).wait_send()

        @pl.when(has_left & (k >= z))
        def _():
            tile_left(k, c).wait_send()

        @pl.when(k > z)
        def _():
            sum_right(k, c).wait_send()

        @pl.when(k < z)
        def _():
            sum_left(k, c).wait_send()

        return carry

    lax.fori_loop(0, DEPTH * PIECES, close_tiles, 0)


def slide_rows(
    tile_cls,
    ln_gain,
    ln_bias,
    gate_weight,
    up_weight,
    down_weight,
    layer_scale,
    final_gain,
    final_bias,
    proj_weight,
    proj_bias,
    slot,
    slide_lengths,
    attn_gain,
    attn_bias,
    q_weight,
    k_weight,
    v_weight,
    o_weight,
):
    seq_count = lax.axis_size("seq")
    across = seq_count // DEPTH
    devices = lax.axis_size("grp") * lax.axis_size("seq")
    rows, width = tile_cls.shape
    count = gate_weight.shape[0]
    narrow = proj_weight.shape[1]
    places = devices * max(16, 2 * rows // devices)
    messages = pltpu.VMEM((DEPTH - 1, rows, width), jnp.bfloat16)
    exchange = pltpu.VMEM((places, narrow), jnp.bfloat16)
    codes = pltpu.VMEM((devices, places // 128, 128), jnp.float32)
    sem = pltpu.SemaphoreType.DMA
    flops = 6 * DEPTH * rows * across * count * width
    anywhere = pl.BlockSpec(memory_space=pl.ANY)
    inside = pl.BlockSpec(memory_space=pltpu.VMEM)
    return pl.pallas_call(
        functools.partial(ffn_kernel, across),
        out_shape=jax.ShapeDtypeStruct((rows, narrow), jnp.bfloat16),
        in_specs=[anywhere, inside, inside, anywhere, anywhere, anywhere]
        + [inside] * 3
        + [anywhere]
        + [inside] * 4
        + [pl.BlockSpec(memory_space=pltpu.SMEM)]
        + [anywhere] * 4,
        out_specs=inside,
        scratch_shapes=[
            pltpu.VMEM((rows, width), jnp.bfloat16),
            pltpu.VMEM((DEPTH, rows, width), jnp.bfloat16),
            pltpu.VMEM((across, 3, count, width), jnp.bfloat16),
            pltpu.VMEM((DEPTH, rows, width), jnp.float32),
            messages,
            messages,
            messages,
            messages,
            pltpu.VMEM((rows, narrow), jnp.bfloat16),
            exchange,
            exchange,
            codes,
            codes,
            pltpu.VMEM((1, rows), jnp.int32),
            pltpu.VMEM((width, narrow), jnp.bfloat16),
            pltpu.VMEM((4, narrow, narrow), jnp.bfloat16),
            pltpu.VMEM((W_SEG // rows, rows, narrow), jnp.bfloat16),
            pltpu.VMEM((rows, narrow), jnp.float32),
            pltpu.VMEM((rows, narrow), jnp.bfloat16),
            pltpu.VMEM((rows, narrow), jnp.bfloat16),
            pltpu.VMEM((rows, narrow), jnp.bfloat16),
            pltpu.VMEM((rows, rows), jnp.float32),
            pltpu.VMEM((HEADS, HEAD_DIM, rows), jnp.float32),
            pltpu.VMEM((HEADS, 1, rows), jnp.float32),
            pltpu.VMEM((HEADS, 1, rows), jnp.float32),
            pltpu.VMEM((rows // RATE, 2 * narrow), jnp.bfloat16),
            pltpu.VMEM((seq_count * rows // RATE, 2 * narrow), jnp.bfloat16),
            sem((9,)),
            sem((2, DEPTH, PIECES)),
            sem((DEPTH, PIECES)),
            sem((across, 3, 2)),
            sem((across, 3, 2)),
            sem((across, 3, 2)),
            sem((across, 3, 2)),
            sem((across, 3, 2, 2)),
            sem((across, 3, 2, 2)),
            sem((DEPTH - 1, PIECES)),
            sem((DEPTH - 1, PIECES)),
            sem((DEPTH - 1, PIECES)),
            sem((DEPTH - 1, PIECES)),
            sem((devices,)),
            sem((devices,)),
            sem((devices,)),
            sem((devices,)),
            sem((3, 2)),
            sem((W_SEG // rows, 2)),
            sem((seq_count,)),
            sem((seq_count,)),
        ],
        compiler_params=pltpu.CompilerParams(
            collective_id=0, has_side_effects=True, vmem_limit_bytes=60 << 20
        ),
        cost_estimate=pl.CostEstimate(
            flops=flops, bytes_accessed=6 * count * width, transcendentals=0
        ),
    )(
        tile_cls,
        ln_gain,
        ln_bias,
        gate_weight,
        up_weight,
        down_weight,
        layer_scale,
        final_gain,
        final_bias,
        proj_weight,
        proj_bias,
        slot,
        attn_gain,
        attn_bias,
        slide_lengths,
        q_weight,
        k_weight,
        v_weight,
        o_weight,
    )


def local(*arrays):
    return slide_rows(*arrays)[None]


def solution(mesh):
    return jax.shard_map(
        local,
        mesh=mesh,
        in_specs=(
            P(("grp", "seq"), None),
            P(),
            P(),
            P("seq", None),
            P("seq", None),
            P("seq", None),
            P(),
            P(),
            P(),
            P(),
            P(),
            P(("grp", "seq")),
            P("grp", None),
            P(),
            P(),
            P(),
            P(),
            P(),
            P(),
        ),
        out_specs=P("grp", "seq", None),
        check_vma=False,
    )
```

```python
import functools

import jax
import jax.numpy as jnp
from jax import lax
from jax.experimental import pallas as pl
from jax.experimental.pallas import tpu as pltpu
from jax.sharding import PartitionSpec as P

HEADS = 12
HEAD_DIM = 64
W_SEG = 1024
RATE = 16
DEPTH = 4
PIECES = 4
QUAD = 4


def normalise(values, gain_vec, bias_vector):
    average = jnp.mean(values, -1, keepdims=True)
    centred = values - average
    variance = jnp.mean(centred * centred, -1, keepdims=True)
    return centred * lax.rsqrt(variance + 1e-06) * gain_vec + bias_vector


def ffn_kernel(
    across,
    cls_ref,
    ln_gain_ref,
    ln_bias_ref,
    gate_ref,
    up_ref,
    down_ref,
    scale_ref,
    final_gain_ref,
    final_bias_ref,
    proj_ref,
    proj_bias_ref,
    slot_ref,
    attn_gain_ref,
    attn_bias_ref,
    lengths_ref,
    q_ref,
    k_ref,
    v_ref,
    o_ref,
    out_ref,
    resid,
    tiles,
    weights,
    sums,
    right_out,
    left_out,
    right_in,
    left_in,
    embed,
    outgoing,
    arrived,
    codes_out,
    codes_in,
    bucket,
    proj,
    square,
    normed,
    placed,
    queries,
    keys,
    values,
    bias,
    total,
    peak,
    weight,
    far_out,
    far_in,
    held,
    held_turned,
    local_sem,
    tile_send,
    tile_recv,
    y_send,
    y_recv,
    x_send,
    x_recv,
    twin_send,
    twin_recv,
    right_send,
    right_recv,
    left_send,
    left_recv,
    code_send,
    code_recv,
    row_send,
    row_recv,
    near_send,
    near_recv,
    far_send,
    far_recv,
):
    seq = lax.axis_index("seq")
    grp = lax.axis_index("grp")
    z = seq // across
    y = seq % across
    member = grp % QUAD
    twin = grp + 1 - 2 * (grp % 2)
    beside = grp + 2 - 4 * (member // 2)
    last = DEPTH - 1
    has_right = z < last
    has_left = z > 0
    rows = resid.shape[0]
    piece = rows // PIECES
    count = gate_ref.shape[0]
    part = count // (2 * QUAD)
    own = (gate_ref, up_ref, down_ref)
    messages = 6 * (across - 1)

    def y_peer(r):
        return {"seq": z * across + (y + r) % across}

    seq_count = lax.axis_size("seq")
    devices = lax.axis_size("grp") * seq_count
    here = grp * seq_count + seq
    places = outgoing.shape[0]
    capacity = places // devices

    def peer(r):
        there = (here + r) % devices
        return there, {"grp": there // seq_count, "seq": there % seq_count}

    barrier = pltpu.get_barrier_semaphore()

    def greet(r, carry):
        pl.semaphore_signal(barrier, inc=1, device_id=peer(r)[1])
        return carry

    lax.fori_loop(1, devices, greet, 0)

    cls_load = pltpu.make_async_copy(cls_ref, resid, local_sem.at[3])
    cls_load.start()
    loads = [
        pltpu.make_async_copy(own[i], weights.at[0, i], local_sem.at[i]) for i in range(3)
    ]
    loads.append(pltpu.make_async_copy(proj_ref, proj, local_sem.at[4]))
    squares = (q_ref, k_ref, v_ref, o_ref)
    loads += [
        pltpu.make_async_copy(squares[i], square.at[i], local_sem.at[5 + i]) for i in range(4)
    ]
    for load in loads:
        load.start()

    def unit_rows(who, h):
        return pl.ds(pl.multiple_of((2 * who + h) * part, part), part)

    def where_is(w):
        return 1 + w // 6, w // 2 % 3, w % 2

    def y_copy(w):
        r, i, h = where_is(w)
        unit = weights.at[r, i, unit_rows(member, h)]
        return pltpu.make_async_remote_copy(
            src_ref=unit,
            dst_ref=unit,
            send_sem=y_send.at[r, i, h],
            recv_sem=y_recv.at[r, i, h],
            device_id=y_peer(r),
        )

    def x_copy(w, who):
        r, i, h = where_is(w)
        unit = weights.at[r, i, unit_rows(who, h)]
        return pltpu.make_async_remote_copy(
            src_ref=unit,
            dst_ref=unit,
            send_sem=x_send.at[r, i, h],
            recv_sem=x_recv.at[r, i, h],
            device_id={"grp": beside},
        )

    def twin_copy(w, hop, who):
        r, i, h = where_is(w)
        unit = weights.at[r, i, unit_rows(who, h)]
        return pltpu.make_async_remote_copy(
            src_ref=unit,
            dst_ref=unit,
            send_sem=twin_send.at[r, i, h, hop],
            recv_sem=twin_recv.at[r, i, h, hop],
            device_id={"grp": twin},
        )

    over = (member + 2) % QUAD
    twin_member = member + 1 - 2 * (member % 2)
    twin_over = (twin_member + 2) % QUAD

    def rows_of(c):
        return pl.ds(pl.multiple_of(c * piece, piece), piece)

    cls_load.wait()

    def tile_right(k, c):
        unit = tiles.at[k, rows_of(c)]
        return pltpu.make_async_remote_copy(
            src_ref=unit,
            dst_ref=unit,
            send_sem=tile_send.at[0, k, c],
            recv_sem=tile_recv.at[k, c],
            device_id={"seq": seq + across},
        )

    def tile_left(k, c):
        unit = tiles.at[k, rows_of(c)]
        return pltpu.make_async_remote_copy(
            src_ref=unit,
            dst_ref=unit,
            send_sem=tile_send.at[1, k, c],
            recv_sem=tile_recv.at[k, c],
            device_id={"seq": seq - across},
        )

    def norm_piece(c, carry):
        values = resid[rows_of(c)].astype(jnp.float32)
        tiles[z, rows_of(c)] = normalise(
            values, ln_gain_ref[...], ln_bias_ref[...]
        ).astype(jnp.bfloat16)
        return carry

    lax.fori_loop(0, PIECES, norm_piece, 0)
    pl.semaphore_wait(barrier, devices - 1)

    for r in range(1, across):
        for i in range(3):
            for h in range(2):
                pltpu.make_async_remote_copy(
                    src_ref=own[i].at[unit_rows(member, h)],
                    dst_ref=weights.at[r, i, unit_rows(member, h)],
                    send_sem=y_send.at[r, i, h],
                    recv_sem=y_recv.at[r, i, h],
                    device_id=y_peer(r),
                ).start()

    for c in range(PIECES):

        @pl.when((z == 0) | (has_right & (c < z)))
        def _():
            tile_right(z, c).start()

        @pl.when((z == last) | (has_left & (c < last - z)))
        def _():
            tile_left(z, c).start()

    targets = slot_ref[...].reshape(1, rows) // rows
    spots = slot_ref[...].reshape(1, rows) % rows
    ordinal = lax.broadcasted_iota(jnp.int32, (places, rows), 0)
    def code_copy(r):
        there, device_id = peer(r)
        return pltpu.make_async_remote_copy(
            src_ref=codes_out.at[there],
            dst_ref=codes_in.at[here],
            send_sem=code_send.at[there],
            recv_sem=code_recv.at[here],
            device_id=device_id,
        )

    def code_start(r, carry):
        code_copy(r).start()
        return carry

    def send_codes():
        device_iota = lax.broadcasted_iota(jnp.int32, (devices, rows), 0)
        chosen = device_iota == targets
        before = (
            lax.broadcasted_iota(jnp.int32, (rows, rows), 0)
            < lax.broadcasted_iota(jnp.int32, (rows, rows), 1)
        ).astype(jnp.bfloat16)
        earlier = jnp.dot(chosen.astype(jnp.bfloat16), before, preferred_element_type=jnp.float32)
        rank = jnp.sum(jnp.where(chosen, earlier, 0.0), 0, keepdims=True).astype(jnp.int32)
        bucket[...] = targets * capacity + rank
        coded = jnp.where(chosen, spots + 1, 0).astype(jnp.bfloat16)
        codes = lax.dot_general(
            coded,
            (ordinal == here * capacity + rank).astype(jnp.bfloat16),
            (((1,), (1,)), ((), ())),
            preferred_element_type=jnp.float32,
        )
        for j in range(places // 128):
            codes_out[:, j, :] = codes[:, 128 * j : 128 * (j + 1)]
        codes_in[here] = codes_out[here]
        lax.fori_loop(1, devices, code_start, 0)

    def tile_step(p):
        q = p - 2 + z
        k, c = last - q // PIECES, q % PIECES
        live = (q >= 0) & (q < PIECES * DEPTH)

        @pl.when(live & (k > z))
        def _():
            tile_left(k, c).wait_recv()

        @pl.when(live & (k > z) & has_left)
        def _():
            tile_left(k, c).start()

        @pl.when(live & (k == z) & (c == 0) & has_left & has_right)
        def _():
            for e in range(PIECES):

                @pl.when(e >= last - z)
                def _():
                    tile_left(z, e).start()

        s = p + 1 - z
        m, d = s // PIECES, s % PIECES
        there = (s >= 0) & (s < PIECES * DEPTH)

        @pl.when(there & (m < z))
        def _():
            tile_right(m, d).wait_recv()

        @pl.when(there & (m < z) & has_right)
        def _():
            tile_right(m, d).start()

        @pl.when(there & (m == z) & (d == 0) & has_left & has_right)
        def _():
            for e in range(PIECES):

                @pl.when(e >= z)
                def _():
                    tile_right(z, e).start()

    def settle(w, carry):
        twin_copy(w, 0, twin_member).wait_recv()
        twin_copy(w, 1, twin_over).wait_recv()
        return carry

    def sum_right(k, c):
        return pltpu.make_async_remote_copy(
            src_ref=right_out.at[k - 1, rows_of(c)],
            dst_ref=right_in.at[k - 1, rows_of(c)],
            send_sem=right_send.at[k - 1, c],
            recv_sem=right_recv.at[k - 1, c],
            device_id={"seq": seq + across},
        )

    def sum_left(k, c):
        return pltpu.make_async_remote_copy(
            src_ref=left_out.at[k, rows_of(c)],
            dst_ref=left_in.at[k, rows_of(c)],
            send_sem=left_send.at[k, c],
            recv_sem=left_recv.at[k, c],
            device_id={"seq": seq - across},
        )

    def relay_right(k, c):
        sum_right(k, c).wait_recv()
        right_out[k - 1, rows_of(c)] = (
            sums[k, rows_of(c)] + right_in[k - 1, rows_of(c)].astype(jnp.float32)
        ).astype(jnp.bfloat16)
        sum_right(k, c).start()

    def relay_left(k, c):
        sum_left(k, c).wait_recv()
        left_out[k, rows_of(c)] = (
            sums[k, rows_of(c)] + left_in[k, rows_of(c)].astype(jnp.float32)
        ).astype(jnp.bfloat16)
        sum_left(k, c).start()

    is_end = (z == 0) | (z == last)
    ready = max(6, messages)

    def pick(n, values):
        found = values[0]
        for i in range(1, len(values)):
            found = jnp.where(n == i, values[i], found)
        return found

    first = jnp.where(z < 2, last, 0)
    second = jnp.where(z == 0, 2, jnp.where(z == 1, 0, jnp.where(z == 2, last, 1)))
    third = jnp.where(z == 0, 1, jnp.where(z == 1, 2, jnp.where(z == 2, 1, 2)))
    end_plan = [
        (1, z, 0, 1),
        (5, first, 0, 1),
        (ready, first, 1, across),
        (ready + 3, second, 0, across),
        (ready + 7, third, 0, across),
        (ready + 8, z, 1, across),
    ]
    mid_plan = [
        (1, z, 0, 1),
        (4, first, 0, 1),
        (5, second, 0, 1),
        (ready, first, 1, across),
        (ready + 1, second, 1, across),
        (ready + 2, third, 0, across),
        (ready + 4, z, 1, across),
    ]

    def chosen_work(p):
        k, low, high = z, 0, 0
        for plan, live in ((end_plan, is_end), (mid_plan, ~is_end)):
            for at, tile, start, stop in plan:
                hit = live & (p == at)
                k = jnp.where(hit, tile, k)
                low = jnp.where(hit, start, low)
                high = jnp.where(hit, stop, high)
        return k, low, high

    def step(p, carry):
        @pl.when((p >= 0) & (p < messages))
        def _():
            y_copy(p).wait_recv()
            x_copy(p, member).start()
            twin_copy(p, 0, member).start()

        @pl.when((p >= 1) & (p <= messages))
        def _():
            x_copy(p - 1, over).wait_recv()
            twin_copy(p - 1, 1, over).start()

        tile_step(p)

        @pl.when(p == 0)
        def _():
            for load in loads:
                load.wait()

            send_codes()

        @pl.when(p == 2)
        def _():
            square[2] = jnp.transpose(square[2])
            held[...] = (
                lax.broadcasted_iota(jnp.int32, held.shape, 0) % RATE
                == lax.broadcasted_iota(jnp.int32, held.shape, 1) // HEAD_DIM
            ).astype(jnp.bfloat16)
            held_turned[...] = (
                lax.broadcasted_iota(jnp.int32, held_turned.shape, 1) % RATE
                == lax.broadcasted_iota(jnp.int32, held_turned.shape, 0) // HEAD_DIM
            ).astype(jnp.bfloat16)

        @pl.when(p == ready)
        def _():
            lax.fori_loop(0, messages, settle, 0)

        u = p - ready - 2
        v = u - 1

        @pl.when((z == 1) & (u >= 0) & (u < 2 * PIECES))
        def _():
            relay_right(last - u // PIECES, u % PIECES)

        @pl.when((z == 2) & (u >= 0) & (u < 2 * PIECES))
        def _():
            relay_left(u // PIECES, u % PIECES)

        @pl.when((z == 1) & (v >= 0) & (v < PIECES))
        def _():
            relay_left(0, v)

        @pl.when((z == 2) & (v >= 0) & (v < PIECES))
        def _():
            relay_right(last, v)

        k, low, high = chosen_work(p)

        def shard(r, inner):
            tile = tiles[k]
            dims = (((1,), (1,)), ((), ()))
            gate = lax.dot_general(
                tile, weights[r, 0], dims, preferred_element_type=jnp.float32
            )
            up_part = lax.dot_general(
                tile, weights[r, 1], dims, preferred_element_type=jnp.float32
            )
            hidden = (gate / (1.0 + jnp.exp(-gate)) * up_part).astype(jnp.bfloat16)
            term = jnp.dot(hidden, weights[r, 2], preferred_element_type=jnp.float32)

            @pl.when(r == 0)
            def _():
                sums[k] = term

            @pl.when(r > 0)
            def _():
                sums[k] += term

            return inner

        lax.fori_loop(low, high, shard, 0)
        done = (low < high) & (high == across) & (k != z)

        @pl.when((z == 0) & done)
        def _():
            right_out[k - 1] = sums[k].astype(jnp.bfloat16)
            for c in range(PIECES):
                sum_right(k, c).start()

        @pl.when((z == last) & done)
        def _():
            left_out[k] = sums[k].astype(jnp.bfloat16)
            for c in range(PIECES):
                sum_left(k, c).start()

        return carry

    lax.fori_loop(-1, ready + 10, step, 0)

    def finish(c, carry):
        @pl.when(has_left)
        def _():
            sum_right(z, c).wait_recv()
            sums[z, rows_of(c)] += right_in[z - 1, rows_of(c)].astype(jnp.float32)

        @pl.when(has_right)
        def _():
            sum_left(z, c).wait_recv()
            sums[z, rows_of(c)] += left_in[z, rows_of(c)].astype(jnp.float32)

        tile_out = resid[rows_of(c)].astype(jnp.float32) + scale_ref[...] * sums[z, rows_of(c)]
        final = normalise(tile_out, final_gain_ref[...], final_bias_ref[...]).astype(jnp.bfloat16)
        embed[rows_of(c)] = (
            jnp.dot(final, proj[...], preferred_element_type=jnp.float32) + proj_bias_ref[...]
        ).astype(jnp.bfloat16)
        return carry

    lax.fori_loop(0, PIECES, finish, 0)

    sends = (ordinal == bucket[...]).astype(jnp.bfloat16)
    outgoing[...] = jnp.dot(sends, embed[...], preferred_element_type=jnp.float32).astype(
        jnp.bfloat16
    )

    def slab(device):
        return pl.ds(pl.multiple_of(device * capacity, capacity), capacity)

    def row_copy(r):
        there, device_id = peer(r)
        return pltpu.make_async_remote_copy(
            src_ref=outgoing.at[slab(there)],
            dst_ref=arrived.at[slab(here)],
            send_sem=row_send.at[there],
            recv_sem=row_recv.at[here],
            device_id=device_id,
        )

    def row_start(r, carry):
        row_copy(r).start()
        return carry

    lax.fori_loop(1, devices, row_start, 0)
    arrived[slab(here)] = outgoing[slab(here)]

    def collect(r, carry):
        there, device_id = peer(r)
        pltpu.make_async_remote_copy(
            src_ref=codes_out.at[there],
            dst_ref=codes_in.at[there],
            send_sem=code_send.at[there],
            recv_sem=code_recv.at[there],
            device_id=device_id,
        ).wait_recv()
        pltpu.make_async_remote_copy(
            src_ref=outgoing.at[slab(there)],
            dst_ref=arrived.at[slab(there)],
            send_sem=row_send.at[there],
            recv_sem=row_recv.at[there],
            device_id=device_id,
        ).wait_recv()
        return carry

    lax.fori_loop(1, devices, collect, 0)
    landing = jnp.sum(codes_in[...], 0).astype(jnp.int32) - 1
    targets_iota = lax.broadcasted_iota(jnp.int32, (rows, 128), 0)
    spread = jnp.zeros(placed.shape, jnp.float32)
    for j in range(places // 128):
        lands = (targets_iota == landing[j : j + 1]).astype(jnp.bfloat16)
        spread += jnp.dot(
            lands, arrived[128 * j : 128 * (j + 1)], preferred_element_type=jnp.float32
        )
    placed[...] = spread
    normed[0] = normalise(spread, attn_gain_ref[...], attn_bias_ref[...]).astype(jnp.bfloat16)

    half = rows // 2
    span = W_SEG // rows
    width = placed.shape[1]
    near_one = seq + 1 - 2 * (seq % 2)
    near_two = seq + 2 - 4 * (seq // 2 % 2)
    near_both = near_one + 2 - 4 * (seq // 2 % 2)

    def near_copy(source, kind, h, spot, device):
        there = pl.ds(h * half, half)
        return pltpu.make_async_remote_copy(
            src_ref=normed.at[source, there],
            dst_ref=normed.at[spot, there],
            send_sem=near_send.at[kind, h],
            recv_sem=near_recv.at[spot, h],
            device_id={"seq": device},
        )

    to_one = [near_copy(0, 0, h, 1, near_one) for h in range(2)]
    to_two = [near_copy(0, 1, h, 2, near_two) for h in range(2)]
    passed = [near_copy(1, 2, 0, 3, near_two), near_copy(2, 2, 1, 3, near_one)]
    for copy in (to_one[0], to_two[1], to_one[1], to_two[0]):
        copy.start()

    chosen_rows = rows // RATE

    def far_rows(device):
        return pl.ds(pl.multiple_of(device * chosen_rows, chosen_rows), chosen_rows)

    blocks = seq_count // span
    strangers = seq_count - span

    def stranger(j):
        return (seq // span + 1 + j // span) % blocks * span + (seq + j) % span

    def far_copy(r):
        there = stranger(r)
        return pltpu.make_async_remote_copy(
            src_ref=far_out,
            dst_ref=far_in.at[far_rows(seq)],
            send_sem=far_send.at[there],
            recv_sem=far_recv.at[seq],
            device_id={"seq": there},
        )

    def slides(spots):
        end = lengths_ref[0, 0]
        found = (spots >= end).astype(jnp.int32)
        for j in range(1, lengths_ref.shape[1]):
            end += lengths_ref[0, j]
            found += (spots >= end).astype(jnp.int32)
        return found

    query_pos = seq * rows + lax.broadcasted_iota(jnp.int32, (1, rows), 1)
    query_slide = slides(query_pos)
    query = (
        jnp.dot(normed[0], square[0], preferred_element_type=jnp.float32).astype(jnp.bfloat16)
        * HEAD_DIM ** (-0.5)
    ).astype(jnp.bfloat16)
    half_of = lax.broadcasted_iota(jnp.int32, (rows, width), 1) // HEAD_DIM % 2
    for which in range(2):
        queries[which] = jnp.where(half_of == which, query, jnp.zeros_like(query))
    total[...] = jnp.zeros_like(total)
    weight[...] = jnp.zeros_like(weight)
    peak[...] = jnp.full(peak.shape, -1e30, jnp.float32)
    over_keys = (((1,), (1,)), ((), ()))

    def absorb(keys_of, turned_of, mask_of, count):
        ones = jnp.ones((16, count), jnp.bfloat16)

        def score(head):
            cols = slice(head // 2 * 128, head // 2 * 128 + 128)
            return lax.dot_general(
                keys_of(cols),
                queries[head % 2, :, cols],
                over_keys,
                preferred_element_type=jnp.float32,
            )

        def settle_head(head, share, shrink):
            mixed = jnp.dot(
                jnp.concatenate([turned_of(head), ones], 0),
                share,
                preferred_element_type=jnp.float32,
            )
            total[head] = total[head] * shrink + mixed[:HEAD_DIM]
            weight[head] = weight[head] * shrink + mixed[HEAD_DIM : HEAD_DIM + 1]

        scores = score(0)
        waiting = None
        for head in range(HEADS):
            masked = mask_of(head, scores)
            if head + 1 < HEADS:
                scores = score(head + 1)
            old = peak[head]
            new = jnp.maximum(old, jnp.max(masked, 0, keepdims=True))
            shrink = jnp.exp(old - new)
            share = jnp.exp(masked - new).astype(jnp.bfloat16)
            peak[head] = new
            if waiting is not None:
                settle_head(*waiting)
            waiting = (head, share, shrink)
        settle_head(*waiting)

    def head_rows(head):
        return slice(head * HEAD_DIM, (head + 1) * HEAD_DIM)

    def near_block(r, carry):
        @pl.when(r == 1)
        def _():
            to_one[1].wait_recv()

        @pl.when(r == 2)
        def _():
            to_two[0].wait_recv()

        @pl.when(r == 3)
        def _():
            near_copy(0, 2, 0, 3, near_two).wait_recv()
            near_copy(0, 2, 1, 3, near_one).wait_recv()

        block = normed[r]
        keys[...] = jnp.dot(block, square[1], preferred_element_type=jnp.float32).astype(
            jnp.bfloat16
        )
        values[...] = lax.dot_general(
            square[2], block, over_keys, preferred_element_type=jnp.float32
        ).astype(jnp.bfloat16)

        there = jnp.where(
            r == 0, seq, jnp.where(r == 1, near_one, jnp.where(r == 2, near_two, near_both))
        )
        gather = (
            lax.broadcasted_iota(jnp.int32, (chosen_rows, rows), 0)
            == lax.broadcasted_iota(jnp.int32, (chosen_rows, rows), 1) // RATE
        ).astype(jnp.bfloat16)
        far_in[far_rows(there), :width] = jnp.dot(
            gather, keys[...] * held[...], preferred_element_type=jnp.float32
        ).astype(jnp.bfloat16)
        far_in[far_rows(there), width:] = lax.dot_general(
            gather, values[...] * held_turned[...], over_keys, preferred_element_type=jnp.float32
        ).astype(jnp.bfloat16)

        @pl.when(r == 0)
        def _():
            far_out[...] = far_in[far_rows(seq)]

            def far_start(j, inner):
                far_copy(j).start()
                return inner

            lax.fori_loop(0, strangers, far_start, 0)

        key_pos = there * rows + lax.broadcasted_iota(jnp.int32, (rows, 1), 0)
        bias[...] = jnp.where(query_slide == slides(key_pos), 0.0, -1e30)
        absorb(
            lambda cols: keys[:, cols],
            lambda head: values[head_rows(head)],
            lambda head, scores: scores + bias[...],
            rows,
        )

        @pl.when(r == 0)
        def _():
            to_one[0].wait_recv()
            passed[0].start()
            to_two[1].wait_recv()
            passed[1].start()

        return carry

    lax.fori_loop(0, span, near_block, 0)

    def far_collect(r, carry):
        there = stranger(r)
        pltpu.make_async_remote_copy(
            src_ref=far_out,
            dst_ref=far_in.at[far_rows(there)],
            send_sem=far_send.at[there],
            recv_sem=far_recv.at[there],
            device_id={"seq": there},
        ).wait_recv()
        return carry

    lax.fori_loop(0, strangers, far_collect, 0)
    far_pos = RATE * lax.broadcasted_iota(jnp.int32, (far_in.shape[0], 1), 0)

    def far_mask(head, scores):
        seen = (query_slide == slides(far_pos + head)) & (query_pos % RATE == head)
        return jnp.where(seen, scores, -1e30)

    far_turned = jnp.transpose(far_in[:, width:])
    absorb(
        lambda cols: far_in[:, cols],
        lambda head: far_turned[head_rows(head)],
        far_mask,
        far_in.shape[0],
    )

    attn = (total[...] / weight[...]).astype(jnp.bfloat16).reshape(width, rows)
    out_ref[...] = (
        placed[...]
        + lax.dot_general(
            attn, square[3], (((0,), (0,)), ((), ())), preferred_element_type=jnp.float32
        )
    ).astype(jnp.bfloat16)

    for copy in to_one + to_two + passed:
        copy.wait_send()

    def close_far(r, carry):
        far_copy(r).wait_send()
        return carry

    lax.fori_loop(0, strangers, close_far, 0)

    def close_rows(r, carry):
        code_copy(r).wait_send()
        row_copy(r).wait_send()
        return carry

    lax.fori_loop(1, devices, close_rows, 0)

    def close_weights(w, carry):
        y_copy(w).wait_send()
        x_copy(w, member).wait_send()
        twin_copy(w, 0, member).wait_send()
        twin_copy(w, 1, over).wait_send()
        return carry

    lax.fori_loop(0, messages, close_weights, 0)

    def close_tiles(u, carry):
        k, c = u // PIECES, u % PIECES

        @pl.when(has_right & (k <= z))
        def _():
            tile_right(k, c).wait_send()

        @pl.when(has_left & (k >= z))
        def _():
            tile_left(k, c).wait_send()

        @pl.when(k > z)
        def _():
            sum_right(k, c).wait_send()

        @pl.when(k < z)
        def _():
            sum_left(k, c).wait_send()

        return carry

    lax.fori_loop(0, DEPTH * PIECES, close_tiles, 0)


def slide_rows(
    tile_cls,
    ln_gain,
    ln_bias,
    gate_weight,
    up_weight,
    down_weight,
    layer_scale,
    final_gain,
    final_bias,
    proj_weight,
    proj_bias,
    slot,
    slide_lengths,
    attn_gain,
    attn_bias,
    q_weight,
    k_weight,
    v_weight,
    o_weight,
):
    seq_count = lax.axis_size("seq")
    across = seq_count // DEPTH
    devices = lax.axis_size("grp") * lax.axis_size("seq")
    rows, width = tile_cls.shape
    count = gate_weight.shape[0]
    narrow = proj_weight.shape[1]
    places = devices * max(16, 2 * rows // devices)
    messages = pltpu.VMEM((DEPTH - 1, rows, width), jnp.bfloat16)
    exchange = pltpu.VMEM((places, narrow), jnp.bfloat16)
    codes = pltpu.VMEM((devices, places // 128, 128), jnp.float32)
    sem = pltpu.SemaphoreType.DMA
    flops = 6 * DEPTH * rows * across * count * width
    anywhere = pl.BlockSpec(memory_space=pl.ANY)
    inside = pl.BlockSpec(memory_space=pltpu.VMEM)
    return pl.pallas_call(
        functools.partial(ffn_kernel, across),
        out_shape=jax.ShapeDtypeStruct((rows, narrow), jnp.bfloat16),
        in_specs=[anywhere, inside, inside, anywhere, anywhere, anywhere]
        + [inside] * 3
        + [anywhere]
        + [inside] * 4
        + [pl.BlockSpec(memory_space=pltpu.SMEM)]
        + [anywhere] * 4,
        out_specs=inside,
        scratch_shapes=[
            pltpu.VMEM((rows, width), jnp.bfloat16),
            pltpu.VMEM((DEPTH, rows, width), jnp.bfloat16),
            pltpu.VMEM((across, 3, count, width), jnp.bfloat16),
            pltpu.VMEM((DEPTH, rows, width), jnp.float32),
            messages,
            messages,
            messages,
            messages,
            pltpu.VMEM((rows, narrow), jnp.bfloat16),
            exchange,
            exchange,
            codes,
            codes,
            pltpu.VMEM((1, rows), jnp.int32),
            pltpu.VMEM((width, narrow), jnp.bfloat16),
            pltpu.VMEM((4, narrow, narrow), jnp.bfloat16),
            pltpu.VMEM((W_SEG // rows, rows, narrow), jnp.bfloat16),
            pltpu.VMEM((rows, narrow), jnp.float32),
            pltpu.VMEM((2, rows, narrow), jnp.bfloat16),
            pltpu.VMEM((rows, narrow), jnp.bfloat16),
            pltpu.VMEM((narrow, rows), jnp.bfloat16),
            pltpu.VMEM((rows, rows), jnp.float32),
            pltpu.VMEM((HEADS, HEAD_DIM, rows), jnp.float32),
            pltpu.VMEM((HEADS, 1, rows), jnp.float32),
            pltpu.VMEM((HEADS, 1, rows), jnp.float32),
            pltpu.VMEM((rows // RATE, 2 * narrow), jnp.bfloat16),
            pltpu.VMEM((seq_count * rows // RATE, 2 * narrow), jnp.bfloat16),
            pltpu.VMEM((rows, narrow), jnp.bfloat16),
            pltpu.VMEM((narrow, rows), jnp.bfloat16),
            sem((9,)),
            sem((2, DEPTH, PIECES)),
            sem((DEPTH, PIECES)),
            sem((across, 3, 2)),
            sem((across, 3, 2)),
            sem((across, 3, 2)),
            sem((across, 3, 2)),
            sem((across, 3, 2, 2)),
            sem((across, 3, 2, 2)),
            sem((DEPTH - 1, PIECES)),
            sem((DEPTH - 1, PIECES)),
            sem((DEPTH - 1, PIECES)),
            sem((DEPTH - 1, PIECES)),
            sem((devices,)),
            sem((devices,)),
            sem((devices,)),
            sem((devices,)),
            sem((3, 2)),
            sem((W_SEG // rows, 2)),
            sem((seq_count,)),
            sem((seq_count,)),
        ],
        compiler_params=pltpu.CompilerParams(
            collective_id=0, has_side_effects=True, vmem_limit_bytes=60 << 20
        ),
        cost_estimate=pl.CostEstimate(
            flops=flops, bytes_accessed=6 * count * width, transcendentals=0
        ),
    )(
        tile_cls,
        ln_gain,
        ln_bias,
        gate_weight,
        up_weight,
        down_weight,
        layer_scale,
        final_gain,
        final_bias,
        proj_weight,
        proj_bias,
        slot,
        attn_gain,
        attn_bias,
        slide_lengths,
        q_weight,
        k_weight,
        v_weight,
        o_weight,
    )


def local(*arrays):
    return slide_rows(*arrays)[None]


def solution(mesh):
    return jax.shard_map(
        local,
        mesh=mesh,
        in_specs=(
            P(("grp", "seq"), None),
            P(),
            P(),
            P("seq", None),
            P("seq", None),
            P("seq", None),
            P(),
            P(),
            P(),
            P(),
            P(),
            P(("grp", "seq")),
            P("grp", None),
            P(),
            P(),
            P(),
            P(),
            P(),
            P(),
        ),
        out_specs=P("grp", "seq", None),
        check_vma=False,
    )
```

```python
import functools

import jax
import jax.numpy as jnp
from jax import lax
from jax.experimental import pallas as pl
from jax.experimental.pallas import tpu as pltpu
from jax.sharding import PartitionSpec as P

HEADS = 12
HEAD_DIM = 64
W_SEG = 1024
RATE = 16
DEPTH = 4
PIECES = 4
QUAD = 4


def normalise(values, gain_vec, bias_vector):
    average = jnp.mean(values, -1, keepdims=True)
    centred = values - average
    variance = jnp.mean(centred * centred, -1, keepdims=True)
    return centred * lax.rsqrt(variance + 1e-06) * gain_vec + bias_vector


def ffn_kernel(
    across,
    cls_ref,
    ln_gain_ref,
    ln_bias_ref,
    gate_ref,
    up_ref,
    down_ref,
    scale_ref,
    final_gain_ref,
    final_bias_ref,
    proj_ref,
    proj_bias_ref,
    slot_ref,
    attn_gain_ref,
    attn_bias_ref,
    lengths_ref,
    q_ref,
    k_ref,
    v_ref,
    o_ref,
    out_ref,
    resid,
    tiles,
    weights,
    sums,
    right_out,
    left_out,
    right_in,
    left_in,
    embed,
    outgoing,
    arrived,
    codes_out,
    codes_in,
    bucket,
    proj,
    square,
    normed,
    placed,
    queries,
    keys,
    values,
    bias,
    total,
    peak,
    weight,
    far_out,
    far_in,
    held,
    held_turned,
    local_sem,
    tile_send,
    tile_recv,
    y_send,
    y_recv,
    x_send,
    x_recv,
    twin_send,
    twin_recv,
    right_send,
    right_recv,
    left_send,
    left_recv,
    code_send,
    code_recv,
    row_send,
    row_recv,
    near_send,
    near_recv,
    far_send,
    far_recv,
):
    seq = lax.axis_index("seq")
    grp = lax.axis_index("grp")
    z = seq // across
    y = seq % across
    member = grp % QUAD
    twin = grp + 1 - 2 * (grp % 2)
    beside = grp + 2 - 4 * (member // 2)
    last = DEPTH - 1
    has_right = z < last
    has_left = z > 0
    rows = resid.shape[0]
    piece = rows // PIECES
    count = gate_ref.shape[0]
    part = count // (2 * QUAD)
    own = (gate_ref, up_ref, down_ref)
    messages = 6 * (across - 1)

    def y_peer(r):
        return {"seq": z * across + (y + r) % across}

    seq_count = lax.axis_size("seq")
    devices = lax.axis_size("grp") * seq_count
    here = grp * seq_count + seq
    places = outgoing.shape[0]
    capacity = places // devices

    def peer(r):
        there = (here + r) % devices
        return there, {"grp": there // seq_count, "seq": there % seq_count}

    barrier = pltpu.get_barrier_semaphore()

    def greet(r, carry):
        pl.semaphore_signal(barrier, inc=1, device_id=peer(r)[1])
        return carry

    lax.fori_loop(1, devices, greet, 0)

    cls_load = pltpu.make_async_copy(cls_ref, resid, local_sem.at[3])
    cls_load.start()
    loads = [
        pltpu.make_async_copy(own[i], weights.at[0, i], local_sem.at[i]) for i in range(3)
    ]
    loads.append(pltpu.make_async_copy(proj_ref, proj, local_sem.at[4]))
    squares = (q_ref, k_ref, v_ref, o_ref)
    loads += [
        pltpu.make_async_copy(squares[i], square.at[i], local_sem.at[5 + i]) for i in range(4)
    ]
    for load in loads:
        load.start()

    def unit_rows(who, h):
        return pl.ds(pl.multiple_of((2 * who + h) * part, part), part)

    def where_is(w):
        return 1 + w // 6, w // 2 % 3, w % 2

    def y_copy(w):
        r, i, h = where_is(w)
        unit = weights.at[r, i, unit_rows(member, h)]
        return pltpu.make_async_remote_copy(
            src_ref=unit,
            dst_ref=unit,
            send_sem=y_send.at[r, i, h],
            recv_sem=y_recv.at[r, i, h],
            device_id=y_peer(r),
        )

    def x_copy(w, who):
        r, i, h = where_is(w)
        unit = weights.at[r, i, unit_rows(who, h)]
        return pltpu.make_async_remote_copy(
            src_ref=unit,
            dst_ref=unit,
            send_sem=x_send.at[r, i, h],
            recv_sem=x_recv.at[r, i, h],
            device_id={"grp": beside},
        )

    def twin_copy(w, hop, who):
        r, i, h = where_is(w)
        unit = weights.at[r, i, unit_rows(who, h)]
        return pltpu.make_async_remote_copy(
            src_ref=unit,
            dst_ref=unit,
            send_sem=twin_send.at[r, i, h, hop],
            recv_sem=twin_recv.at[r, i, h, hop],
            device_id={"grp": twin},
        )

    over = (member + 2) % QUAD
    twin_member = member + 1 - 2 * (member % 2)
    twin_over = (twin_member + 2) % QUAD

    def rows_of(c):
        return pl.ds(pl.multiple_of(c * piece, piece), piece)

    cls_load.wait()

    def tile_right(k, c):
        unit = tiles.at[k, rows_of(c)]
        return pltpu.make_async_remote_copy(
            src_ref=unit,
            dst_ref=unit,
            send_sem=tile_send.at[0, k, c],
            recv_sem=tile_recv.at[k, c],
            device_id={"seq": seq + across},
        )

    def tile_left(k, c):
        unit = tiles.at[k, rows_of(c)]
        return pltpu.make_async_remote_copy(
            src_ref=unit,
            dst_ref=unit,
            send_sem=tile_send.at[1, k, c],
            recv_sem=tile_recv.at[k, c],
            device_id={"seq": seq - across},
        )

    def norm_piece(c, carry):
        values = resid[rows_of(c)].astype(jnp.float32)
        tiles[z, rows_of(c)] = normalise(
            values, ln_gain_ref[...], ln_bias_ref[...]
        ).astype(jnp.bfloat16)
        return carry

    lax.fori_loop(0, PIECES, norm_piece, 0)
    pl.semaphore_wait(barrier, devices - 1)

    for r in range(1, across):
        for i in range(3):
            for h in range(2):
                pltpu.make_async_remote_copy(
                    src_ref=own[i].at[unit_rows(member, h)],
                    dst_ref=weights.at[r, i, unit_rows(member, h)],
                    send_sem=y_send.at[r, i, h],
                    recv_sem=y_recv.at[r, i, h],
                    device_id=y_peer(r),
                ).start()

    for c in range(PIECES):

        @pl.when((z == 0) | (has_right & (c < z)))
        def _():
            tile_right(z, c).start()

        @pl.when((z == last) | (has_left & (c < last - z)))
        def _():
            tile_left(z, c).start()

    targets = slot_ref[...].reshape(1, rows) // rows
    spots = slot_ref[...].reshape(1, rows) % rows
    ordinal = lax.broadcasted_iota(jnp.int32, (places, rows), 0)
    def code_copy(r):
        there, device_id = peer(r)
        return pltpu.make_async_remote_copy(
            src_ref=codes_out.at[there],
            dst_ref=codes_in.at[here],
            send_sem=code_send.at[there],
            recv_sem=code_recv.at[here],
            device_id=device_id,
        )

    def code_start(r, carry):
        code_copy(r).start()
        return carry

    def send_codes():
        device_iota = lax.broadcasted_iota(jnp.int32, (devices, rows), 0)
        chosen = device_iota == targets
        before = (
            lax.broadcasted_iota(jnp.int32, (rows, rows), 0)
            < lax.broadcasted_iota(jnp.int32, (rows, rows), 1)
        ).astype(jnp.bfloat16)
        earlier = jnp.dot(chosen.astype(jnp.bfloat16), before, preferred_element_type=jnp.float32)
        rank = jnp.sum(jnp.where(chosen, earlier, 0.0), 0, keepdims=True).astype(jnp.int32)
        bucket[...] = targets * capacity + rank
        coded = jnp.where(chosen, spots + 1, 0).astype(jnp.bfloat16)
        codes = lax.dot_general(
            coded,
            (ordinal == here * capacity + rank).astype(jnp.bfloat16),
            (((1,), (1,)), ((), ())),
            preferred_element_type=jnp.float32,
        )
        for j in range(places // 128):
            codes_out[:, j, :] = codes[:, 128 * j : 128 * (j + 1)]
        codes_in[here] = codes_out[here]
        lax.fori_loop(1, devices, code_start, 0)

    def tile_step(p):
        q = p - 2 + z
        k, c = last - q // PIECES, q % PIECES
        live = (q >= 0) & (q < PIECES * DEPTH)

        @pl.when(live & (k > z))
        def _():
            tile_left(k, c).wait_recv()

        @pl.when(live & (k > z) & has_left)
        def _():
            tile_left(k, c).start()

        @pl.when(live & (k == z) & (c == 0) & has_left & has_right)
        def _():
            for e in range(PIECES):

                @pl.when(e >= last - z)
                def _():
                    tile_left(z, e).start()

        s = p + 1 - z
        m, d = s // PIECES, s % PIECES
        there = (s >= 0) & (s < PIECES * DEPTH)

        @pl.when(there & (m < z))
        def _():
            tile_right(m, d).wait_recv()

        @pl.when(there & (m < z) & has_right)
        def _():
            tile_right(m, d).start()

        @pl.when(there & (m == z) & (d == 0) & has_left & has_right)
        def _():
            for e in range(PIECES):

                @pl.when(e >= z)
                def _():
                    tile_right(z, e).start()

    def settle(w, carry):
        twin_copy(w, 0, twin_member).wait_recv()
        twin_copy(w, 1, twin_over).wait_recv()
        return carry

    def sum_right(k, c):
        return pltpu.make_async_remote_copy(
            src_ref=right_out.at[k - 1, rows_of(c)],
            dst_ref=right_in.at[k - 1, rows_of(c)],
            send_sem=right_send.at[k - 1, c],
            recv_sem=right_recv.at[k - 1, c],
            device_id={"seq": seq + across},
        )

    def sum_left(k, c):
        return pltpu.make_async_remote_copy(
            src_ref=left_out.at[k, rows_of(c)],
            dst_ref=left_in.at[k, rows_of(c)],
            send_sem=left_send.at[k, c],
            recv_sem=left_recv.at[k, c],
            device_id={"seq": seq - across},
        )

    def relay_right(k, c):
        sum_right(k, c).wait_recv()
        right_out[k - 1, rows_of(c)] = (
            sums[k, rows_of(c)] + right_in[k - 1, rows_of(c)].astype(jnp.float32)
        ).astype(jnp.bfloat16)
        sum_right(k, c).start()

    def relay_left(k, c):
        sum_left(k, c).wait_recv()
        left_out[k, rows_of(c)] = (
            sums[k, rows_of(c)] + left_in[k, rows_of(c)].astype(jnp.float32)
        ).astype(jnp.bfloat16)
        sum_left(k, c).start()

    is_end = (z == 0) | (z == last)
    ready = max(6, messages)

    def pick(n, values):
        found = values[0]
        for i in range(1, len(values)):
            found = jnp.where(n == i, values[i], found)
        return found

    first = jnp.where(z < 2, last, 0)
    second = jnp.where(z == 0, 2, jnp.where(z == 1, 0, jnp.where(z == 2, last, 1)))
    third = jnp.where(z == 0, 1, jnp.where(z == 1, 2, jnp.where(z == 2, 1, 2)))
    end_plan = [
        (1, z, 0, 1),
        (5, first, 0, 1),
        (ready, first, 1, across),
        (ready + 3, second, 0, across),
        (ready + 7, third, 0, across),
        (ready + 8, z, 1, across),
    ]
    mid_plan = [
        (1, z, 0, 1),
        (4, first, 0, 1),
        (5, second, 0, 1),
        (ready, first, 1, across),
        (ready + 1, second, 1, across),
        (ready + 2, third, 0, across),
        (ready + 4, z, 1, across),
    ]

    def chosen_work(p):
        k, low, high = z, 0, 0
        for plan, live in ((end_plan, is_end), (mid_plan, ~is_end)):
            for at, tile, start, stop in plan:
                hit = live & (p == at)
                k = jnp.where(hit, tile, k)
                low = jnp.where(hit, start, low)
                high = jnp.where(hit, stop, high)
        return k, low, high

    def step(p, carry):
        @pl.when((p >= 0) & (p < messages))
        def _():
            y_copy(p).wait_recv()
            x_copy(p, member).start()
            twin_copy(p, 0, member).start()

        @pl.when((p >= 1) & (p <= messages))
        def _():
            x_copy(p - 1, over).wait_recv()
            twin_copy(p - 1, 1, over).start()

        tile_step(p)

        @pl.when(p == 0)
        def _():
            for load in loads:
                load.wait()

            send_codes()

        @pl.when(p == 2)
        def _():
            square[2] = jnp.transpose(square[2])
            held[...] = (
                lax.broadcasted_iota(jnp.int32, held.shape, 0) % RATE
                == lax.broadcasted_iota(jnp.int32, held.shape, 1) // HEAD_DIM
            ).astype(jnp.bfloat16)
            held_turned[...] = (
                lax.broadcasted_iota(jnp.int32, held_turned.shape, 1) % RATE
                == lax.broadcasted_iota(jnp.int32, held_turned.shape, 0) // HEAD_DIM
            ).astype(jnp.bfloat16)

        @pl.when(p == ready)
        def _():
            lax.fori_loop(0, messages, settle, 0)

        u = p - ready - 2
        v = u - 1

        @pl.when((z == 1) & (u >= 0) & (u < 2 * PIECES))
        def _():
            relay_right(last - u // PIECES, u % PIECES)

        @pl.when((z == 2) & (u >= 0) & (u < 2 * PIECES))
        def _():
            relay_left(u // PIECES, u % PIECES)

        @pl.when((z == 1) & (v >= 0) & (v < PIECES))
        def _():
            relay_left(0, v)

        @pl.when((z == 2) & (v >= 0) & (v < PIECES))
        def _():
            relay_right(last, v)

        k, low, high = chosen_work(p)

        def shard(r, inner):
            tile = tiles[k]
            dims = (((1,), (1,)), ((), ()))
            gate = lax.dot_general(
                tile, weights[r, 0], dims, preferred_element_type=jnp.float32
            )
            up_part = lax.dot_general(
                tile, weights[r, 1], dims, preferred_element_type=jnp.float32
            )
            hidden = (gate / (1.0 + jnp.exp(-gate)) * up_part).astype(jnp.bfloat16)
            term = jnp.dot(hidden, weights[r, 2], preferred_element_type=jnp.float32)

            @pl.when(r == 0)
            def _():
                sums[k] = term

            @pl.when(r > 0)
            def _():
                sums[k] += term

            return inner

        lax.fori_loop(low, high, shard, 0)
        done = (low < high) & (high == across) & (k != z)

        @pl.when((z == 0) & done)
        def _():
            right_out[k - 1] = sums[k].astype(jnp.bfloat16)
            for c in range(PIECES):
                sum_right(k, c).start()

        @pl.when((z == last) & done)
        def _():
            left_out[k] = sums[k].astype(jnp.bfloat16)
            for c in range(PIECES):
                sum_left(k, c).start()

        return carry

    lax.fori_loop(-1, ready + 10, step, 0)

    def finish(c, carry):
        @pl.when(has_left)
        def _():
            sum_right(z, c).wait_recv()
            sums[z, rows_of(c)] += right_in[z - 1, rows_of(c)].astype(jnp.float32)

        @pl.when(has_right)
        def _():
            sum_left(z, c).wait_recv()
            sums[z, rows_of(c)] += left_in[z, rows_of(c)].astype(jnp.float32)

        tile_out = resid[rows_of(c)].astype(jnp.float32) + scale_ref[...] * sums[z, rows_of(c)]
        final = normalise(tile_out, final_gain_ref[...], final_bias_ref[...]).astype(jnp.bfloat16)
        embed[rows_of(c)] = (
            jnp.dot(final, proj[...], preferred_element_type=jnp.float32) + proj_bias_ref[...]
        ).astype(jnp.bfloat16)
        return carry

    lax.fori_loop(0, PIECES, finish, 0)

    sends = (ordinal == bucket[...]).astype(jnp.bfloat16)
    outgoing[...] = jnp.dot(sends, embed[...], preferred_element_type=jnp.float32).astype(
        jnp.bfloat16
    )

    def slab(device):
        return pl.ds(pl.multiple_of(device * capacity, capacity), capacity)

    def row_copy(r):
        there, device_id = peer(r)
        return pltpu.make_async_remote_copy(
            src_ref=outgoing.at[slab(there)],
            dst_ref=arrived.at[slab(here)],
            send_sem=row_send.at[there],
            recv_sem=row_recv.at[here],
            device_id=device_id,
        )

    def row_start(r, carry):
        row_copy(r).start()
        return carry

    lax.fori_loop(1, devices, row_start, 0)
    arrived[slab(here)] = outgoing[slab(here)]

    def collect(r, carry):
        there, device_id = peer(r)
        pltpu.make_async_remote_copy(
            src_ref=codes_out.at[there],
            dst_ref=codes_in.at[there],
            send_sem=code_send.at[there],
            recv_sem=code_recv.at[there],
            device_id=device_id,
        ).wait_recv()
        pltpu.make_async_remote_copy(
            src_ref=outgoing.at[slab(there)],
            dst_ref=arrived.at[slab(there)],
            send_sem=row_send.at[there],
            recv_sem=row_recv.at[there],
            device_id=device_id,
        ).wait_recv()
        return carry

    lax.fori_loop(1, devices, collect, 0)
    landing = jnp.sum(codes_in[...], 0).astype(jnp.int32) - 1
    targets_iota = lax.broadcasted_iota(jnp.int32, (rows, 128), 0)
    spread = jnp.zeros(placed.shape, jnp.float32)
    for j in range(places // 128):
        lands = (targets_iota == landing[j : j + 1]).astype(jnp.bfloat16)
        spread += jnp.dot(
            lands, arrived[128 * j : 128 * (j + 1)], preferred_element_type=jnp.float32
        )
    placed[...] = spread
    normed[0] = normalise(spread, attn_gain_ref[...], attn_bias_ref[...]).astype(jnp.bfloat16)

    half = rows // 2
    span = W_SEG // rows
    width = placed.shape[1]
    near_one = seq + 1 - 2 * (seq % 2)
    near_two = seq + 2 - 4 * (seq // 2 % 2)
    near_both = near_one + 2 - 4 * (seq // 2 % 2)

    def near_copy(source, kind, h, spot, side, device):
        return pltpu.make_async_remote_copy(
            src_ref=normed.at[source, pl.ds(h * half, half)],
            dst_ref=normed.at[spot, pl.ds(side * half, half)],
            send_sem=near_send.at[kind, h],
            recv_sem=near_recv.at[spot, side],
            device_id={"seq": device},
        )

    to_one = [near_copy(0, 0, 0, 1, 0, near_one), near_copy(0, 0, 1, 2, 1, near_one)]
    to_two = [near_copy(0, 1, 0, 2, 0, near_two), near_copy(0, 1, 1, 1, 1, near_two)]
    passed = [near_copy(1, 2, 0, 3, 0, near_two), near_copy(1, 2, 1, 3, 1, near_one)]
    for copy in (to_one[0], to_two[1], to_one[1], to_two[0]):
        copy.start()

    chosen_rows = rows // RATE

    def far_rows(device):
        return pl.ds(pl.multiple_of(device * chosen_rows, chosen_rows), chosen_rows)

    blocks = seq_count // span
    strangers = seq_count - span

    def stranger(j):
        return (seq // span + 1 + j // span) % blocks * span + (seq + j) % span

    def far_copy(r):
        there = stranger(r)
        return pltpu.make_async_remote_copy(
            src_ref=far_out,
            dst_ref=far_in.at[far_rows(seq)],
            send_sem=far_send.at[there],
            recv_sem=far_recv.at[seq],
            device_id={"seq": there},
        )

    def slides(spots):
        end = lengths_ref[0, 0]
        found = (spots >= end).astype(jnp.int32)
        for j in range(1, lengths_ref.shape[1]):
            end += lengths_ref[0, j]
            found += (spots >= end).astype(jnp.int32)
        return found

    query_pos = seq * rows + lax.broadcasted_iota(jnp.int32, (1, rows), 1)
    query_slide = slides(query_pos)
    query = (
        jnp.dot(normed[0], square[0], preferred_element_type=jnp.float32).astype(jnp.bfloat16)
        * HEAD_DIM ** (-0.5)
    ).astype(jnp.bfloat16)
    half_of = lax.broadcasted_iota(jnp.int32, (rows, width), 1) // HEAD_DIM % 2
    for which in range(2):
        queries[which] = jnp.where(half_of == which, query, jnp.zeros_like(query))
    total[...] = jnp.zeros_like(total)
    weight[...] = jnp.zeros_like(weight)
    peak[...] = jnp.full(peak.shape, -1e30, jnp.float32)
    over_keys = (((1,), (1,)), ((), ()))

    def absorb(keys_of, turned_of, mask_of, count):
        ones = jnp.ones((16, count), jnp.bfloat16)

        def score(head):
            cols = slice(head // 2 * 128, head // 2 * 128 + 128)
            return lax.dot_general(
                keys_of(cols),
                queries[head % 2, :, cols],
                over_keys,
                preferred_element_type=jnp.float32,
            )

        def settle_head(head, share, shrink):
            mixed = jnp.dot(
                jnp.concatenate([turned_of(head), ones], 0),
                share,
                preferred_element_type=jnp.float32,
            )
            total[head] = total[head] * shrink + mixed[:HEAD_DIM]
            weight[head] = weight[head] * shrink + mixed[HEAD_DIM : HEAD_DIM + 1]

        scores = score(0)
        waiting = None
        for head in range(HEADS):
            masked = mask_of(head, scores)
            if head + 1 < HEADS:
                scores = score(head + 1)
            old = peak[head]
            new = jnp.maximum(old, jnp.max(masked, 0, keepdims=True))
            shrink = jnp.exp(old - new)
            share = jnp.exp(masked - new).astype(jnp.bfloat16)
            peak[head] = new
            if waiting is not None:
                settle_head(*waiting)
            waiting = (head, share, shrink)
        settle_head(*waiting)

    def head_rows(head):
        return slice(head * HEAD_DIM, (head + 1) * HEAD_DIM)

    def near_block(r, carry):
        @pl.when(r == 2)
        def _():
            to_two[0].wait_recv()
            to_one[1].wait_recv()

        @pl.when(r == 3)
        def _():
            passed[0].wait_recv()
            passed[1].wait_recv()

        block = normed[r]
        keys[...] = jnp.dot(block, square[1], preferred_element_type=jnp.float32).astype(
            jnp.bfloat16
        )
        values[...] = lax.dot_general(
            square[2], block, over_keys, preferred_element_type=jnp.float32
        ).astype(jnp.bfloat16)

        there = jnp.where(
            r == 0, seq, jnp.where(r == 1, near_one, jnp.where(r == 2, near_two, near_both))
        )
        gather = (
            lax.broadcasted_iota(jnp.int32, (chosen_rows, rows), 0)
            == lax.broadcasted_iota(jnp.int32, (chosen_rows, rows), 1) // RATE
        ).astype(jnp.bfloat16)
        far_in[far_rows(there), :width] = jnp.dot(
            gather, keys[...] * held[...], preferred_element_type=jnp.float32
        ).astype(jnp.bfloat16)
        far_in[far_rows(there), width:] = lax.dot_general(
            gather, values[...] * held_turned[...], over_keys, preferred_element_type=jnp.float32
        ).astype(jnp.bfloat16)

        @pl.when(r == 0)
        def _():
            far_out[...] = far_in[far_rows(seq)]

            def far_start(j, inner):
                far_copy(j).start()
                return inner

            lax.fori_loop(0, strangers, far_start, 0)

        upper = jnp.where(r == 1, near_two, jnp.where(r == 2, near_one, there))
        key_row = lax.broadcasted_iota(jnp.int32, (rows, 1), 0)
        key_pos = jnp.where(key_row < half, there, upper) * rows + key_row
        bias[...] = jnp.where(query_slide == slides(key_pos), 0.0, -1e30)
        absorb(
            lambda cols: keys[:, cols],
            lambda head: values[head_rows(head)],
            lambda head, scores: scores + bias[...],
            rows,
        )

        @pl.when(r == 0)
        def _():
            to_one[0].wait_recv()
            passed[0].start()
            to_two[1].wait_recv()
            passed[1].start()

        return carry

    lax.fori_loop(0, span, near_block, 0)

    def far_collect(r, carry):
        there = stranger(r)
        pltpu.make_async_remote_copy(
            src_ref=far_out,
            dst_ref=far_in.at[far_rows(there)],
            send_sem=far_send.at[there],
            recv_sem=far_recv.at[there],
            device_id={"seq": there},
        ).wait_recv()
        return carry

    lax.fori_loop(0, strangers, far_collect, 0)
    far_row = lax.broadcasted_iota(jnp.int32, (far_in.shape[0], 1), 0)
    far_device, far_index = far_row // chosen_rows, far_row % chosen_rows
    swapped = jnp.where(
        far_device == near_one, near_two, jnp.where(far_device == near_two, near_one, far_device)
    )
    far_device = jnp.where(far_index < chosen_rows // 2, far_device, swapped)
    far_pos = far_device * rows + RATE * far_index

    def far_mask(head, scores):
        seen = (query_slide == slides(far_pos + head)) & (query_pos % RATE == head)
        return jnp.where(seen, scores, -1e30)

    far_turned = jnp.transpose(far_in[:, width:])
    absorb(
        lambda cols: far_in[:, cols],
        lambda head: far_turned[head_rows(head)],
        far_mask,
        far_in.shape[0],
    )

    attn = (total[...] / weight[...]).astype(jnp.bfloat16).reshape(width, rows)
    out_ref[...] = (
        placed[...]
        + lax.dot_general(
            attn, square[3], (((0,), (0,)), ((), ())), preferred_element_type=jnp.float32
        )
    ).astype(jnp.bfloat16)

    for copy in to_one + to_two + passed:
        copy.wait_send()

    def close_far(r, carry):
        far_copy(r).wait_send()
        return carry

    lax.fori_loop(0, strangers, close_far, 0)

    def close_rows(r, carry):
        code_copy(r).wait_send()
        row_copy(r).wait_send()
        return carry

    lax.fori_loop(1, devices, close_rows, 0)

    def close_weights(w, carry):
        y_copy(w).wait_send()
        x_copy(w, member).wait_send()
        twin_copy(w, 0, member).wait_send()
        twin_copy(w, 1, over).wait_send()
        return carry

    lax.fori_loop(0, messages, close_weights, 0)

    def close_tiles(u, carry):
        k, c = u // PIECES, u % PIECES

        @pl.when(has_right & (k <= z))
        def _():
            tile_right(k, c).wait_send()

        @pl.when(has_left & (k >= z))
        def _():
            tile_left(k, c).wait_send()

        @pl.when(k > z)
        def _():
            sum_right(k, c).wait_send()

        @pl.when(k < z)
        def _():
            sum_left(k, c).wait_send()

        return carry

    lax.fori_loop(0, DEPTH * PIECES, close_tiles, 0)


def slide_rows(
    tile_cls,
    ln_gain,
    ln_bias,
    gate_weight,
    up_weight,
    down_weight,
    layer_scale,
    final_gain,
    final_bias,
    proj_weight,
    proj_bias,
    slot,
    slide_lengths,
    attn_gain,
    attn_bias,
    q_weight,
    k_weight,
    v_weight,
    o_weight,
):
    seq_count = lax.axis_size("seq")
    across = seq_count // DEPTH
    devices = lax.axis_size("grp") * lax.axis_size("seq")
    rows, width = tile_cls.shape
    count = gate_weight.shape[0]
    narrow = proj_weight.shape[1]
    places = devices * max(16, 2 * rows // devices)
    messages = pltpu.VMEM((DEPTH - 1, rows, width), jnp.bfloat16)
    exchange = pltpu.VMEM((places, narrow), jnp.bfloat16)
    codes = pltpu.VMEM((devices, places // 128, 128), jnp.float32)
    sem = pltpu.SemaphoreType.DMA
    flops = 6 * DEPTH * rows * across * count * width
    anywhere = pl.BlockSpec(memory_space=pl.ANY)
    inside = pl.BlockSpec(memory_space=pltpu.VMEM)
    return pl.pallas_call(
        functools.partial(ffn_kernel, across),
        out_shape=jax.ShapeDtypeStruct((rows, narrow), jnp.bfloat16),
        in_specs=[anywhere, inside, inside, anywhere, anywhere, anywhere]
        + [inside] * 3
        + [anywhere]
        + [inside] * 4
        + [pl.BlockSpec(memory_space=pltpu.SMEM)]
        + [anywhere] * 4,
        out_specs=inside,
        scratch_shapes=[
            pltpu.VMEM((rows, width), jnp.bfloat16),
            pltpu.VMEM((DEPTH, rows, width), jnp.bfloat16),
            pltpu.VMEM((across, 3, count, width), jnp.bfloat16),
            pltpu.VMEM((DEPTH, rows, width), jnp.float32),
            messages,
            messages,
            messages,
            messages,
            pltpu.VMEM((rows, narrow), jnp.bfloat16),
            exchange,
            exchange,
            codes,
            codes,
            pltpu.VMEM((1, rows), jnp.int32),
            pltpu.VMEM((width, narrow), jnp.bfloat16),
            pltpu.VMEM((4, narrow, narrow), jnp.bfloat16),
            pltpu.VMEM((W_SEG // rows, rows, narrow), jnp.bfloat16),
            pltpu.VMEM((rows, narrow), jnp.float32),
            pltpu.VMEM((2, rows, narrow), jnp.bfloat16),
            pltpu.VMEM((rows, narrow), jnp.bfloat16),
            pltpu.VMEM((narrow, rows), jnp.bfloat16),
            pltpu.VMEM((rows, rows), jnp.float32),
            pltpu.VMEM((HEADS, HEAD_DIM, rows), jnp.float32),
            pltpu.VMEM((HEADS, 1, rows), jnp.float32),
            pltpu.VMEM((HEADS, 1, rows), jnp.float32),
            pltpu.VMEM((rows // RATE, 2 * narrow), jnp.bfloat16),
            pltpu.VMEM((seq_count * rows // RATE, 2 * narrow), jnp.bfloat16),
            pltpu.VMEM((rows, narrow), jnp.bfloat16),
            pltpu.VMEM((narrow, rows), jnp.bfloat16),
            sem((9,)),
            sem((2, DEPTH, PIECES)),
            sem((DEPTH, PIECES)),
            sem((across, 3, 2)),
            sem((across, 3, 2)),
            sem((across, 3, 2)),
            sem((across, 3, 2)),
            sem((across, 3, 2, 2)),
            sem((across, 3, 2, 2)),
            sem((DEPTH - 1, PIECES)),
            sem((DEPTH - 1, PIECES)),
            sem((DEPTH - 1, PIECES)),
            sem((DEPTH - 1, PIECES)),
            sem((devices,)),
            sem((devices,)),
            sem((devices,)),
            sem((devices,)),
            sem((3, 2)),
            sem((W_SEG // rows, 2)),
            sem((seq_count,)),
            sem((seq_count,)),
        ],
        compiler_params=pltpu.CompilerParams(
            collective_id=0, has_side_effects=True, vmem_limit_bytes=60 << 20
        ),
        cost_estimate=pl.CostEstimate(
            flops=flops, bytes_accessed=6 * count * width, transcendentals=0
        ),
    )(
        tile_cls,
        ln_gain,
        ln_bias,
        gate_weight,
        up_weight,
        down_weight,
        layer_scale,
        final_gain,
        final_bias,
        proj_weight,
        proj_bias,
        slot,
        attn_gain,
        attn_bias,
        slide_lengths,
        q_weight,
        k_weight,
        v_weight,
        o_weight,
    )


def local(*arrays):
    return slide_rows(*arrays)[None]


def solution(mesh):
    return jax.shard_map(
        local,
        mesh=mesh,
        in_specs=(
            P(("grp", "seq"), None),
            P(),
            P(),
            P("seq", None),
            P("seq", None),
            P("seq", None),
            P(),
            P(),
            P(),
            P(),
            P(),
            P(("grp", "seq")),
            P("grp", None),
            P(),
            P(),
            P(),
            P(),
            P(),
            P(),
        ),
        out_specs=P("grp", "seq", None),
        check_vma=False,
    )
```
